32 devices in a mesh: pb: 8 (over z, y), ka: 4 (over x, core).
Axes of the slice: x: 2, y: 2, z: 4, core: 2. Of those that a mesh axis runs over, the one named last changes fastest.
Arguments:
- query_rows: bfloat16 [4096, 512], P(('pb', 'ka')), may hold values from -8 to 8
- key_rows: bfloat16 [4096, 128], P(('pb', 'ka')), may hold values from -3 to 3
- value_rows: bfloat16 [4096, 128], P(('pb', 'ka')), may hold values from -6 to 6
- outputs: bfloat16 [4096, 512], P(('pb', 'ka')), may hold values from -3 to 3
- out_grads: bfloat16 [4096, 512], P(('pb', 'ka')), may hold values from -6 to 6
- log_totals: float32 [4, 4096], P(None, ('pb', 'ka')), as said below
- selected: int32 [32, 2], P(('pb', 'ka')), may hold values from 0 to 31, as said below
- counts: int32 [32], P(('pb', 'ka')), may hold values from 1 to 2, as said below
Outputs:
- query_grad: float32 [4096, 512], P(('pb', 'ka'))
- key_grad: float32 [4096, 128], P(('pb', 'ka'))
- value_grad: float32 [4096, 128], P(('pb', 'ka'))
The draws below stay inside these ranges and needn't reach their ends.
Inputs may be any that keep to these rules, and one draw needn't show every extreme that they name: log_totals[h, t] is the logarithm of the sum of exp(scores) over all keys that row t of head h attends, with scores and attended keys as in the reference program. `selected`: slot 0 of row q is q itself; the first counts[q] entries of row q are distinct blocks no later than q; entries from slot counts[q] on are padding and are ignored. counts[q] is at most q + 1; the last query block's count is 2.
All inputs are finite; a program needn't handle non-finite values.
Results may differ from the reference program's by a relative error of at most 0.0029.
Values may be sent and summed in bfloat16 or wider, within the bound.
A program may use at most 64 MiB of HBM per device.

```python
import jax
import jax.numpy as jnp
from jax import lax

H = 4
HD = 128
BLK = 128
NB = 32
NSEL = 2


def query_field(key):
    sub_key = jax.random.fold_in(key, 101)
    array_shape = (NB * BLK, H * HD)
    drawn_values = 2.5 * jax.random.truncated_normal(sub_key, -3.2, 3.2, array_shape, jnp.float32)
    return drawn_values.astype(jnp.bfloat16)


def key_field(key):
    sub_key = jax.random.fold_in(key, 202)
    array_shape = (NB * BLK, HD)
    drawn_values = jax.random.truncated_normal(sub_key, -3.0, 3.0, array_shape, jnp.float32)
    return drawn_values.astype(jnp.bfloat16)


def count_field(key):
    sub_key = jax.random.fold_in(key, 303)
    block_index = jnp.arange(NB, dtype=jnp.int32)
    shortfall = jax.random.randint(sub_key, (NB,), 0, NSEL // 2 + 1, dtype=jnp.int32)
    drawn_counts = jnp.minimum(NSEL - shortfall, block_index + 1)
    return jnp.where(block_index == NB - 1, NSEL, drawn_counts).astype(jnp.int32)


def selection_field(key):
    sub_key = jax.random.fold_in(key, 404)
    rows_index = jnp.arange(NB, dtype=jnp.int32)[:, None]
    cols_index = jnp.arange(NB, dtype=jnp.int32)[None, :]
    random_part = jax.random.randint(sub_key, (NB, NB), 0, 131072, dtype=jnp.int32)
    ranking = random_part * NB + cols_index
    ranking = jnp.where(cols_index == rows_index, 131072 * NB + rows_index, ranking)
    ranking = jnp.where(cols_index > rows_index, -1, ranking)
    return lax.top_k(ranking, NSEL)[1].astype(jnp.int32)


def draw_query_rows(key, part):
    return query_field(key)


def draw_key_rows(key, part):
    return key_field(key)


def draw_counts(key, part):
    return count_field(key)


def draw_selected(key, part):
    return selection_field(key)


def draw_log_totals(key, part):
    query_blocks = query_field(key).astype(jnp.float32).reshape(NB, BLK, H, HD)
    key_blocks = key_field(key).astype(jnp.float32).reshape(NB, BLK, HD)
    chosen = selection_field(key)
    valid_counts = count_field(key)
    offsets = jnp.arange(BLK, dtype=jnp.int32)
    slot_index = jnp.arange(NSEL, dtype=jnp.int32)

    def one_block(block_index):
        key_ids = chosen[block_index]
        scores = jnp.einsum('rhd,jcd->hrjc', query_blocks[block_index], key_blocks[key_ids], precision=lax.Precision.HIGHEST) * HD ** (-0.5)
        query_pos = block_index * BLK + offsets
        key_pos = key_ids[:, None] * BLK + offsets[None, :]
        allowed = (slot_index < valid_counts[block_index])[None, :, None] & (key_pos[None, :, :] <= query_pos[:, None, None])
        masked = jnp.where(allowed[None], scores, -1e+30)
        return jax.nn.logsumexp(masked.reshape(H, BLK, NSEL * BLK), axis=2)
    per_block = lax.map(one_block, jnp.arange(NB, dtype=jnp.int32))
    return jnp.transpose(per_block, (1, 0, 2)).reshape(H, NB * BLK).astype(jnp.float32)


def level_of(rng, dims, split, smallest, top_value):
    loudness, own = 1.0, jax.random.fold_in(rng, 6)
    for position, shards_of in split:
        draws = jnp.exp(jax.random.uniform(jax.random.fold_in(own, position), (shards_of,), jnp.float32, smallest / len(split), top_value / len(split)))
        loudness = loudness * jnp.repeat(draws, dims[position] // shards_of).reshape([-1 if axis == position else 1 for axis in range(len(dims))])
    return loudness


def centred(rng, extent, scale, most, split=(), kind=jnp.bfloat16):
    values = scale * jax.random.normal(rng, extent, jnp.float32)
    if split:
        values = values * level_of(rng, extent, split, -0.22, 0.18)
    return jnp.clip(values, -most, most).astype(kind)


def setup_inputs(seed: int = 0) -> dict:
    key_of = jax.random.split(jax.random.key(seed), 9)
    return {
        "query_rows": draw_query_rows(jax.random.fold_in(key_of[8], 71), 0),
        "key_rows": draw_key_rows(jax.random.fold_in(key_of[8], 71), 0),
        "value_rows": centred(key_of[2], (NB * BLK, HD), 1.0, 6.0, ((0, 32),)),
        "outputs": centred(key_of[3], (NB * BLK, H * HD), 0.5, 3.0, ((0, 32),)),
        "out_grads": centred(key_of[4], (NB * BLK, H * HD), 1.0, 6.0, ((0, 32),)),
        "log_totals": draw_log_totals(jax.random.fold_in(key_of[8], 71), 0),
        "selected": draw_selected(jax.random.fold_in(key_of[8], 71), 0),
        "counts": draw_counts(jax.random.fold_in(key_of[8], 71), 0),
    }


HIGHEST_MODE = lax.Precision.HIGHEST


def widen(array_in):
    return array_in.astype(jnp.float32)


def narrow(array_in):
    return lax.optimization_barrier(array_in.astype(jnp.bfloat16)).astype(jnp.float32)


def reference(query_rows, key_rows, value_rows, outputs, out_grads, log_totals, selected, counts):
    seq_rows = NB * BLK
    score_scale = HD ** -0.5
    row_delta = jnp.sum((widen(out_grads) * widen(outputs)).reshape(seq_rows, H, HD), axis=2).T
    key_blocks = key_rows.reshape(NB, BLK, HD)
    value_blocks = value_rows.reshape(NB, BLK, HD)
    slot_index = jnp.arange(NSEL, dtype=jnp.int32)
    offsets = jnp.arange(BLK, dtype=jnp.int32)

    def one_block(key_grads, block_index):
        row_start = block_index * BLK
        key_ids = selected[block_index]
        query_tile = widen(lax.dynamic_slice_in_dim(query_rows, row_start, BLK, 0)).reshape(BLK, H, HD)
        grad_tile = widen(lax.dynamic_slice_in_dim(out_grads, row_start, BLK, 0)).reshape(BLK, H, HD)
        total_tile = lax.dynamic_slice_in_dim(log_totals, row_start, BLK, 1)
        delta_tile = lax.dynamic_slice_in_dim(row_delta, row_start, BLK, 1)
        key_sel = widen(key_blocks[key_ids])
        value_sel = widen(value_blocks[key_ids])
        scores = jnp.einsum("rhd,jcd->hrjc", query_tile, key_sel, precision=HIGHEST_MODE) * score_scale
        query_pos = row_start + offsets
        key_pos = key_ids[:, None] * BLK + offsets[None, :]
        allowed = (slot_index < counts[block_index])[None, :, None] & (key_pos[None, :, :] <= query_pos[:, None, None])
        probs = jnp.exp(jnp.where(allowed[None], scores - total_tile[:, :, None, None], -1e30))
        prob_grads = jnp.einsum("rhd,jcd->hrjc", grad_tile, value_sel, precision=HIGHEST_MODE)
        score_grads = probs * (prob_grads - delta_tile[:, :, None, None])
        rounded_probs = narrow(probs)
        rounded_grads = narrow(score_grads)
        query_part = jnp.einsum("hrjc,jcd->rhd", rounded_grads, key_sel, precision=HIGHEST_MODE) * score_scale
        key_part = jnp.einsum("hrjc,rhd->jcd", rounded_grads, query_tile, precision=HIGHEST_MODE) * score_scale
        value_part = jnp.einsum("hrjc,rhd->jcd", rounded_probs, grad_tile, precision=HIGHEST_MODE)
        key_grads = key_grads.at[key_ids].add(jnp.concatenate([key_part, value_part], 2))
        return key_grads, query_part.reshape(BLK, H * HD)

    start_grads = jnp.zeros((NB, BLK, 2 * HD), jnp.float32)
    key_grads, query_grad = lax.scan(one_block, start_grads, jnp.arange(NB, dtype=jnp.int32))
    query_grad = query_grad.reshape(seq_rows, H * HD)
    key_grads = key_grads.reshape(seq_rows, 2 * HD)
    return query_grad, key_grads[:, :HD], key_grads[:, HD:]
```

```python
import functools

import jax
import jax.numpy as jnp
from jax import lax
from jax.experimental import pallas as pl
from jax.experimental.pallas import tpu as pltpu
from jax.sharding import PartitionSpec as P

VERY_LOW = -1e30


def passed_along(value, axis, steps):
    count = lax.axis_size(axis)
    pairs = [(source, (source + steps) % count) for source in range(count)]
    return lax.ppermute(value, axis, pairs)


def head_sums(grad_rows, out_rows, head_width):
    row_total = grad_rows.shape[0]
    part_heads = grad_rows.shape[1] // head_width
    product = grad_rows.astype(jnp.float32) * out_rows.astype(jnp.float32)
    return jnp.sum(product.reshape(row_total, part_heads, head_width), axis=2).T


def shards(query_rows, key_rows, value_rows, outputs, out_grads, log_totals, selected, counts):
    ka_count = lax.axis_size("ka")
    ka_index = lax.axis_index("ka")
    pb_index = lax.axis_index("pb")
    block_count = selected.shape[0]
    slot_count = selected.shape[1]
    head_width = key_rows.shape[1]
    block_rows = query_rows.shape[0] // block_count
    score_scale = head_width ** (-0.5)
    key_pairs = jnp.concatenate([key_rows, value_rows], 1)
    column_keys = lax.all_gather(key_pairs, "pb", axis=0, tiled=True)
    peer_slots, peer_counts = (
        lax.all_gather(selected, "ka", axis=0, tiled=True),
        lax.all_gather(counts, "ka", axis=0, tiled=True),
    )
    key_grads = jnp.zeros((column_keys.shape[0], 2 * head_width), jnp.float32)
    row_offsets = jnp.arange(block_rows, dtype=jnp.int32)
    flat_owner = jnp.repeat(jnp.arange(block_count, dtype=jnp.int32), slot_count)
    flat_slot = jnp.tile(jnp.arange(slot_count, dtype=jnp.int32), block_count)
    flat_places = jnp.arange(block_count * slot_count, dtype=jnp.int32)

    def visit_block(row_stack, query_grad, stat_stack, anchor, key_grads):
        held_query = row_stack[0]
        held_grad = row_stack[1]
        total_rows = stat_stack[0]
        delta_rows = head_sums(row_stack[1], row_stack[2], head_width)
        part_heads = total_rows.shape[0]
        held_slots = lax.dynamic_slice_in_dim(
            peer_slots, anchor * block_count, block_count, 0
        ).reshape(-1)
        held_counts = jnp.repeat(
            lax.dynamic_slice_in_dim(peer_counts, anchor * block_count, block_count, 0), slot_count
        )
        first_block = (pb_index * ka_count + anchor) * block_count
        wanted = (flat_slot < held_counts) & (held_slots // block_count % ka_count == ka_index)
        earlier = flat_places[None, :] <= flat_places[:, None]
        position = jnp.sum((earlier & wanted[None, :]).astype(jnp.int32), axis=1) - 1
        placed = wanted[:, None] & (position[:, None] == flat_places[None, :])
        packed_ids = jnp.sum(jnp.where(placed, held_slots[:, None], 0), axis=0)
        packed_owner = jnp.sum(jnp.where(placed, flat_owner[:, None], 0), axis=0)
        live_tiles = jnp.sum(wanted.astype(jnp.int32))

        def one_tile(tile_index, loop_state):
            query_grad, key_grads = loop_state
            key_block = packed_ids[tile_index]
            owner_block = packed_owner[tile_index]
            key_start = (
                key_block // (block_count * ka_count) * block_count + key_block % block_count
            ) * block_rows
            pair_tile = lax.dynamic_slice_in_dim(column_keys, key_start, block_rows, 0)
            key_tile = pair_tile[:, :head_width]
            value_tile = pair_tile[:, head_width:]
            query_tile = held_query.reshape(block_rows, part_heads, head_width)
            grad_tile = held_grad.reshape(block_rows, part_heads, head_width)
            scores = (
                jnp.einsum("rhd,cd->hrc", query_tile, key_tile, preferred_element_type=jnp.float32)
                * score_scale
            )
            query_pos = (first_block + owner_block) * block_rows + row_offsets
            key_pos = key_block * block_rows + row_offsets
            allowed = key_pos[None, :] <= query_pos[:, None]
            probs_full = jnp.exp(
                jnp.where(allowed[None], scores - total_rows[:, :, None], VERY_LOW)
            )
            prob_grads = jnp.einsum(
                "rhd,cd->hrc", grad_tile, value_tile, preferred_element_type=jnp.float32
            )
            score_grads = probs_full * (prob_grads - delta_rows[:, :, None])
            rounded_probs = probs_full.astype(jnp.bfloat16)
            rounded_grads = score_grads.astype(jnp.bfloat16)
            value_part = jnp.einsum(
                "hrc,rhd->cd", rounded_probs, grad_tile, preferred_element_type=jnp.float32
            )
            key_part = (
                jnp.einsum(
                    "hrc,rhd->cd", rounded_grads, query_tile, preferred_element_type=jnp.float32
                )
                * score_scale
            )
            query_part = (
                jnp.einsum(
                    "hrc,cd->rhd", rounded_grads, key_tile, preferred_element_type=jnp.float32
                )
                * score_scale
            )
            old_query = query_grad
            query_grad = old_query + query_part.reshape(block_rows, -1)
            old_keys = lax.dynamic_slice_in_dim(key_grads, key_start, block_rows, 0)
            key_grads = lax.dynamic_update_slice_in_dim(
                key_grads, old_keys + jnp.concatenate([key_part, value_part], 1), key_start, 0
            )
            return (query_grad, key_grads)

        return lax.fori_loop(0, live_tiles, one_tile, (query_grad, key_grads))

    query_part = query_rows
    grad_zero = jnp.zeros(query_part.shape, jnp.float32)
    row_stack = jnp.stack([query_part, out_grads, outputs])
    query_grad = grad_zero
    stat_stack = log_totals[None]

    def forward_hop(hop_index, loop_state):
        row_stack, query_grad, stat_stack, key_grads = loop_state
        anchor = (ka_index - hop_index) % ka_count
        query_grad, key_grads = visit_block(row_stack, query_grad, stat_stack, anchor, key_grads)
        row_stack = passed_along(row_stack, "ka", 1)
        query_grad, stat_stack = passed_along((query_grad, stat_stack), "ka", 1)
        return (row_stack, query_grad, stat_stack, key_grads)

    row_stack, query_grad, stat_stack, key_grads = lax.fori_loop(
        0, ka_count - 1, forward_hop, (row_stack, query_grad, stat_stack, key_grads)
    )
    query_grad, key_grads = visit_block(
        row_stack, query_grad, stat_stack, (ka_index + 1) % ka_count, key_grads
    )
    query_grad = passed_along(query_grad, "ka", 1)
    owned_grads = lax.psum_scatter(key_grads, "pb", scatter_dimension=0, tiled=True)
    return (query_grad, owned_grads[:, :head_width], owned_grads[:, head_width:])


MESH = pl.DeviceIdType.MESH
VMEM_BUDGET = 40 << 20


NT = (((1,), (1,)), ((), ()))
TN = (((0,), (0,)), ((), ()))
INFO = 128


def tile_probs(key_tile, query_stack, total_row, allowed, scale):
    scores = lax.dot_general(key_tile, query_stack, NT, preferred_element_type=jnp.float32) * scale
    return jnp.exp(jnp.where(allowed, scores - total_row, VERY_LOW))


def tile_score_grads(probs, value_tile, grad_stack, delta_row):
    prob_grads = lax.dot_general(value_tile, grad_stack, NT, preferred_element_type=jnp.float32)
    return (probs * (prob_grads - delta_row)).astype(jnp.bfloat16)


def query_share(score_grads, key_tile, scale):
    return lax.dot_general(score_grads, key_tile, TN, preferred_element_type=jnp.float32) * scale


def whole_kernel(
    ka_count, inner, line_count,
    query_hbm, key_hbm, value_hbm, out_hbm, grad_hbm, total_hbm, selected_hbm, counts_hbm,
    query_grad_ref, key_grad_ref, value_grad_ref,
    query_ref, out_ref, grad_ref, total_ref, selected_ref, counts_ref,
    key_own, value_own, key_plane, value_column,
    key_picked, value_picked, key_in, value_in,
    key_part, value_part, kgrad_plane, vgrad_column,
    kgrad_sum, vgrad_sum, kgrad_in, vgrad_in,
    own_info, plane_info, column_info, query_stack, grad_stack, query_acc, key_acc, value_acc,
    info_send_p, info_recv_p, info_send_c, info_recv_c,
    key_send_p, key_recv_p, key_send_c, key_recv_c,
    value_send_c, value_recv_c, value_send_p, value_recv_p,
    kgrad_send_p, kgrad_recv_p, kgrad_send_c, kgrad_recv_c,
    vgrad_send_c, vgrad_recv_c, vgrad_send_p, vgrad_recv_p,
    load_sem,
):
    bf, f32 = jnp.bfloat16, jnp.float32
    plane_count = inner * ka_count
    column_count = 2 * line_count
    pb_index, ka_index = lax.axis_index("pb"), lax.axis_index("ka")
    line = lax.div(pb_index, inner)
    row = lax.rem(pb_index, inner)
    place = row * ka_count + ka_index
    chip, core = lax.div(place, 2), lax.rem(place, 2)
    member = line * 2 + core
    block_rows, head_width = key_hbm.shape
    half_rows = block_rows // 2
    heads = total_hbm.shape[0]
    scale = head_width ** (-0.5)
    block = line * plane_count + place

    def half(which):
        return pl.ds(pl.multiple_of(which * half_rows, half_rows), half_rows)

    def partner(me, offset, count):
        if count & (count - 1):
            return lax.rem(me + offset, count)
        peer, bit = me, 1
        while bit < count:
            if offset & bit:
                peer = peer + bit - 2 * bit * lax.rem(lax.div(me, bit), 2)
            bit *= 2
        return peer

    def plane_peer(offset):
        peer = partner(place, offset, plane_count)
        return peer, (line * inner + lax.div(peer, ka_count), lax.rem(peer, ka_count))

    def column_peer(offset):
        peer = partner(member, offset, column_count)
        there = chip * 2 + lax.rem(peer, 2)
        return peer, (lax.div(peer, 2) * inner + lax.div(there, ka_count), lax.rem(there, ka_count))

    plane = [plane_peer(offset) for offset in range(plane_count)]
    column = [column_peer(offset) for offset in range(column_count)]

    barrier = pltpu.get_barrier_semaphore()
    for group in (column, plane):
        for _, device in group[:0:-1]:
            pl.semaphore_signal(barrier, inc=1, device_id=device, device_id_type=MESH)
    loads = [
        pltpu.make_async_copy(source, target, load_sem.at[index])
        for index, (source, target) in enumerate((
            (selected_hbm, selected_ref), (counts_hbm, counts_ref),
            (key_hbm, key_own), (value_hbm, value_own),
            (key_hbm.at[half(core)], key_plane.at[place]), (value_hbm.at[half(core)], value_column.at[member]),
            (query_hbm, query_ref), (grad_hbm, grad_ref), (out_hbm, out_ref), (total_hbm, total_ref),
        ))
    ]
    for load in loads:
        load.start()

    loads[0].wait()
    loads[1].wait()
    target = jnp.where(counts_ref[0] > 1, selected_ref[0, 1], -1)
    own_info[0] = target
    plane_info[place, 0] = target
    column_info[member, 0] = target

    sent = []

    def send(peer, offset, source, target, send_sem, recv_sem, me):
        copy = pltpu.make_async_remote_copy(
            src_ref=source, dst_ref=target, send_sem=send_sem.at[offset], recv_sem=recv_sem.at[me],
            device_id=peer[1], device_id_type=MESH,
        )
        copy.start()
        sent.append(copy)

    def arrive(group, landed, send_sem, recv_sem):
        for offset in range(1, len(group)):
            peer, device = group[offset]
            pltpu.make_async_remote_copy(
                src_ref=landed(peer), dst_ref=landed(peer), send_sem=send_sem.at[offset],
                recv_sem=recv_sem.at[peer], device_id=device, device_id_type=MESH,
            ).wait_recv()

    def farthest_first(group):
        return [(offset, *group[offset]) for offset in range(len(group) - 1, 0, -1)]

    def at_line(ref):
        return lambda peer: ref.at[lax.div(peer, 2), half(lax.rem(peer, 2))]

    for load in loads[2:6]:
        load.wait()
    pl.semaphore_wait(barrier, plane_count + column_count - 2)
    for offset, peer, device in farthest_first(column):
        send((peer, device), offset, own_info, column_info.at[member], info_send_c, info_recv_c, member)
    for offset, peer, device in farthest_first(plane):
        send((peer, device), offset, own_info, plane_info.at[place], info_send_p, info_recv_p, place)
    for offset, peer, device in farthest_first(column):
        send((peer, device), offset, value_own.at[half(lax.rem(peer, 2))], value_column.at[member],
             value_send_c, value_recv_c, member)
    for offset, peer, device in farthest_first(plane):
        send((peer, device), offset, key_own.at[half(lax.rem(peer, 2))], key_plane.at[place],
             key_send_p, key_recv_p, place)

    for load in loads[6:]:
        load.wait()
    deltas = []
    for head in range(heads):
        columns = pl.ds(head * head_width, head_width)
        rows = pl.ds(head * block_rows, block_rows)
        query_stack[rows, :] = query_ref[:, columns]
        grad_stack[rows, :] = grad_ref[:, columns]
        product = grad_ref[:, columns].astype(f32) * out_ref[:, columns].astype(f32)
        deltas.append(jnp.sum(product.T, axis=0, keepdims=True))
    delta_row = jnp.concatenate(deltas, axis=1)
    total_row = jnp.concatenate([total_ref[head : head + 1, :] for head in range(heads)], axis=1)
    stack_shape = (block_rows, heads * block_rows)
    key_offset = lax.broadcasted_iota(jnp.int32, stack_shape, 0)
    query_offset = lax.rem(lax.broadcasted_iota(jnp.int32, stack_shape, 1), block_rows)

    arrive(column, lambda peer: column_info.at[peer], info_send_c, info_recv_c)
    arrive(plane, lambda peer: plane_info.at[peer], info_send_p, info_recv_p)
    plane_targets = [plane_info[peer, 0] for peer, _ in plane]
    column_targets = [column_info[peer, 0] for peer, _ in column]

    arrive(plane, lambda peer: key_plane.at[peer], key_send_p, key_recv_p)
    for offset, peer, device in farthest_first(column):
        key_picked[offset] = key_plane[lax.rem(jnp.maximum(column_targets[offset], 0), plane_count)]
        send((peer, device), offset, key_picked.at[offset], key_in.at[line, half(core)], key_send_c, key_recv_c, member)
    listed = jnp.maximum(target, 0)
    key_in[line, half(core), :] = key_plane[lax.rem(listed, plane_count)]

    arrive(column, lambda peer: value_column.at[peer], value_send_c, value_recv_c)
    for offset, peer, device in farthest_first(plane):
        wanted = jnp.maximum(plane_targets[offset], 0)
        value_picked[offset] = value_column[lax.div(wanted, plane_count) * 2 + lax.rem(wanted, 2)]
        send((peer, device), offset, value_picked.at[offset], value_in.at[chip, half(core)],
             value_send_p, value_recv_p, place)
    value_in[chip, half(core), :] = value_column[lax.div(listed, plane_count) * 2 + lax.rem(listed, 2)]

    own_key = key_own[...]
    probs = tile_probs(own_key, query_stack[...], total_row, key_offset <= query_offset, scale)
    value_acc[...] = jnp.dot(probs.astype(bf), grad_stack[...], preferred_element_type=f32)
    score_grads = tile_score_grads(probs, value_own[...], grad_stack[...], delta_row)
    query_acc[...] = query_share(score_grads, own_key, scale)
    key_acc[...] = jnp.dot(score_grads, query_stack[...], preferred_element_type=f32) * scale

    arrive(column, at_line(key_in), key_send_c, key_recv_c)
    allowed = (key_offset + target * block_rows <= query_offset + block * block_rows) & (
        jnp.full(stack_shape, target, jnp.int32) >= 0
    )
    key_tile = key_in[lax.div(listed, plane_count)]
    probs = tile_probs(key_tile, query_stack[...], total_row, allowed, scale)
    value_part[...] = jnp.dot(probs.astype(bf), grad_stack[...], preferred_element_type=f32).astype(bf)
    for offset, peer, device in farthest_first(column):
        send((peer, device), offset, value_part.at[half(lax.rem(peer, 2))], vgrad_column.at[member],
             vgrad_send_c, vgrad_recv_c, member)
    vgrad_column[member] = value_part[half(core), :]
    arrive(plane, at_line(value_in), value_send_p, value_recv_p)
    score_grads = tile_score_grads(
        probs, value_in[lax.div(lax.rem(listed, plane_count), 2)], grad_stack[...], delta_row
    )
    key_part[...] = (jnp.dot(score_grads, query_stack[...], preferred_element_type=f32) * scale).astype(bf)
    for offset, peer, device in farthest_first(plane):
        send((peer, device), offset, key_part.at[half(lax.rem(peer, 2))], kgrad_plane.at[place],
             kgrad_send_p, kgrad_recv_p, place)
    kgrad_plane[place] = key_part[half(core), :]
    query_acc[...] += query_share(score_grads, key_tile, scale)
    for head in range(heads):
        query_grad_ref[:, pl.ds(head * head_width, head_width)] = query_acc[
            pl.ds(head * block_rows, block_rows), :
        ]

    def total_for(owner, group, targets, held):
        sums = jnp.zeros((half_rows, head_width), f32)
        for (peer, _), aimed in zip(group, targets):
            sums = sums + jnp.where(aimed == owner, held[peer].astype(f32), 0.0)
        return sums.astype(bf)

    arrive(plane, lambda peer: kgrad_plane.at[peer], kgrad_send_p, kgrad_recv_p)
    for offset, peer, device in farthest_first(column):
        owner = lax.div(peer, 2) * plane_count + chip * 2 + lax.rem(peer, 2)
        kgrad_sum[offset] = total_for(owner, plane, plane_targets, kgrad_plane)
        send((peer, device), offset, kgrad_sum.at[offset], kgrad_in.at[line, half(core)],
             kgrad_send_c, kgrad_recv_c, member)
    kgrad_in[line, half(core), :] = total_for(block, plane, plane_targets, kgrad_plane)

    arrive(column, lambda peer: vgrad_column.at[peer], vgrad_send_c, vgrad_recv_c)
    for offset, peer, device in farthest_first(plane):
        owner = line * plane_count + peer
        vgrad_sum[offset] = total_for(owner, column, column_targets, vgrad_column)
        send((peer, device), offset, vgrad_sum.at[offset], vgrad_in.at[chip, half(core)],
             vgrad_send_p, vgrad_recv_p, place)
    vgrad_in[chip, half(core), :] = total_for(block, column, column_targets, vgrad_column)

    arrive(column, at_line(kgrad_in), kgrad_send_c, kgrad_recv_c)
    key_total = key_acc[...]
    for other in range(line_count):
        key_total = key_total + kgrad_in[other].astype(f32)
    key_grad_ref[...] = key_total
    arrive(plane, at_line(vgrad_in), vgrad_send_p, vgrad_recv_p)
    value_total = value_acc[...]
    for other in range(plane_count // 2):
        value_total = value_total + vgrad_in[other].astype(f32)
    value_grad_ref[...] = value_total
    for copy in sent:
        copy.wait_send()


def kernel_shards(query_rows, key_rows, value_rows, outputs, out_grads, log_totals, selected, counts):
    ka_count, pb_count = lax.axis_size("ka"), lax.axis_size("pb")
    inner = 2 if pb_count % 2 == 0 else 1
    line_count, plane_count = pb_count // inner, inner * ka_count
    column_count = 2 * line_count
    block_rows, head_width = key_rows.shape
    heads = log_totals.shape[0]
    tile = key_rows.shape
    part = (block_rows // 2, head_width)
    dma = pltpu.SemaphoreType.DMA
    vmem = pl.BlockSpec(memory_space=pltpu.VMEM)
    hbm = pl.BlockSpec(memory_space=pl.ANY)
    bf, f32 = jnp.bfloat16, jnp.float32
    shapes = (query_rows.shape, key_rows.shape, value_rows.shape)
    plane_then_column = (plane_count, plane_count, column_count, column_count)
    column_then_plane = (column_count, column_count, plane_count, plane_count)
    held = pl.pallas_call(
        functools.partial(whole_kernel, ka_count, inner, line_count),
        out_shape=tuple(pltpu.VMEM(shape, f32) for shape in shapes),
        in_specs=[hbm] * 8,
        out_specs=(vmem, vmem, vmem),
        scratch_shapes=[
            pltpu.VMEM(query_rows.shape, bf),
            pltpu.VMEM(query_rows.shape, bf),
            pltpu.VMEM(query_rows.shape, bf),
            pltpu.VMEM(log_totals.shape, f32),
            pltpu.SMEM(selected.shape, jnp.int32),
            pltpu.SMEM(counts.shape, jnp.int32),
            pltpu.VMEM(tile, bf),
            pltpu.VMEM(tile, bf),
            pltpu.VMEM((plane_count, *part), bf),
            pltpu.VMEM((column_count, *part), bf),
            pltpu.VMEM((column_count, *part), bf),
            pltpu.VMEM((plane_count, *part), bf),
            pltpu.VMEM((line_count, *tile), bf),
            pltpu.VMEM((plane_count // 2, *tile), bf),
            pltpu.VMEM(tile, bf),
            pltpu.VMEM(tile, bf),
            pltpu.VMEM((plane_count, *part), bf),
            pltpu.VMEM((column_count, *part), bf),
            pltpu.VMEM((column_count, *part), bf),
            pltpu.VMEM((plane_count, *part), bf),
            pltpu.VMEM((line_count, *tile), bf),
            pltpu.VMEM((plane_count // 2, *tile), bf),
            pltpu.SMEM((INFO,), jnp.int32),
            pltpu.SMEM((plane_count, INFO), jnp.int32),
            pltpu.SMEM((column_count, INFO), jnp.int32),
            pltpu.VMEM((heads * block_rows, head_width), bf),
            pltpu.VMEM((heads * block_rows, head_width), bf),
            pltpu.VMEM((heads * block_rows, head_width), f32),
            pltpu.VMEM(tile, f32),
            pltpu.VMEM(tile, f32),
            *[dma((count,)) for count in plane_then_column * 2 + column_then_plane + plane_then_column + column_then_plane],
            dma((10,)),
        ],
        compiler_params=pltpu.CompilerParams(collective_id=0, has_side_effects=True),
    )(query_rows, key_rows, value_rows, outputs, out_grads, log_totals, selected, counts)
    return pl.pallas_call(
        write_kernel,
        out_shape=tuple(jax.ShapeDtypeStruct(shape, f32) for shape in shapes),
        in_specs=[vmem] * 3,
        out_specs=(hbm, hbm, hbm),
        scratch_shapes=[dma((3,))],
    )(*[pltpu.with_memory_space_constraint(part, pltpu.VMEM) for part in held])


def write_kernel(*refs):
    sources, targets, sem = refs[:3], refs[3:6], refs[6]
    stores = [pltpu.make_async_copy(*pair, sem.at[i]) for i, pair in enumerate(zip(sources, targets))]
    for store in stores:
        store.start()
    for store in stores:
        store.wait()


def fits_kernel(query_rows, key_rows, value_rows, outputs, out_grads, log_totals, selected, counts):
    pb_count, ka_count = lax.axis_size("pb"), lax.axis_size("ka")
    block_rows, head_width = key_rows.shape
    inner = 2 if pb_count % 2 == 0 else 1
    tile_bytes = 2 * block_rows * head_width
    tiles = 6 * (pb_count // inner + inner * ka_count)
    return (
        selected.shape[0] == 1
        and selected.shape[1] == 2
        and ka_count % 2 == 0
        and pb_count > inner
        and block_rows == head_width == 128
        and tiles * tile_bytes < VMEM_BUDGET
    )


def either(*arrays):
    return kernel_shards(*arrays) if fits_kernel(*arrays) else shards(*arrays)


def solution(mesh):
    return jax.shard_map(
        either,
        mesh=mesh,
        in_specs=(
            P(("pb", "ka"), None),
            P(("pb", "ka"), None),
            P(("pb", "ka"), None),
            P(("pb", "ka"), None),
            P(("pb", "ka"), None),
            P(None, ("pb", "ka")),
            P(("pb", "ka"), None),
            P(("pb", "ka")),
        ),
        out_specs=(P(("pb", "ka"), None), P(("pb", "ka"), None), P(("pb", "ka"), None)),
        check_vma=False,
    )
```

```python
import functools

import jax
import jax.numpy as jnp
from jax import lax
from jax.experimental import pallas as pl
from jax.experimental.pallas import tpu as pltpu
from jax.sharding import PartitionSpec as P

VERY_LOW = -1e30


def passed_along(value, axis, steps):
    count = lax.axis_size(axis)
    pairs = [(source, (source + steps) % count) for source in range(count)]
    return lax.ppermute(value, axis, pairs)


def head_sums(grad_rows, out_rows, head_width):
    row_total = grad_rows.shape[0]
    part_heads = grad_rows.shape[1] // head_width
    product = grad_rows.astype(jnp.float32) * out_rows.astype(jnp.float32)
    return jnp.sum(product.reshape(row_total, part_heads, head_width), axis=2).T


def shards(query_rows, key_rows, value_rows, outputs, out_grads, log_totals, selected, counts):
    ka_count = lax.axis_size("ka")
    ka_index = lax.axis_index("ka")
    pb_index = lax.axis_index("pb")
    block_count = selected.shape[0]
    slot_count = selected.shape[1]
    head_width = key_rows.shape[1]
    block_rows = query_rows.shape[0] // block_count
    score_scale = head_width ** (-0.5)
    key_pairs = jnp.concatenate([key_rows, value_rows], 1)
    column_keys = lax.all_gather(key_pairs, "pb", axis=0, tiled=True)
    peer_slots, peer_counts = (
        lax.all_gather(selected, "ka", axis=0, tiled=True),
        lax.all_gather(counts, "ka", axis=0, tiled=True),
    )
    key_grads = jnp.zeros((column_keys.shape[0], 2 * head_width), jnp.float32)
    row_offsets = jnp.arange(block_rows, dtype=jnp.int32)
    flat_owner = jnp.repeat(jnp.arange(block_count, dtype=jnp.int32), slot_count)
    flat_slot = jnp.tile(jnp.arange(slot_count, dtype=jnp.int32), block_count)
    flat_places = jnp.arange(block_count * slot_count, dtype=jnp.int32)

    def visit_block(row_stack, query_grad, stat_stack, anchor, key_grads):
        held_query = row_stack[0]
        held_grad = row_stack[1]
        total_rows = stat_stack[0]
        delta_rows = head_sums(row_stack[1], row_stack[2], head_width)
        part_heads = total_rows.shape[0]
        held_slots = lax.dynamic_slice_in_dim(
            peer_slots, anchor * block_count, block_count, 0
        ).reshape(-1)
        held_counts = jnp.repeat(
            lax.dynamic_slice_in_dim(peer_counts, anchor * block_count, block_count, 0), slot_count
        )
        first_block = (pb_index * ka_count + anchor) * block_count
        wanted = (flat_slot < held_counts) & (held_slots // block_count % ka_count == ka_index)
        earlier = flat_places[None, :] <= flat_places[:, None]
        position = jnp.sum((earlier & wanted[None, :]).astype(jnp.int32), axis=1) - 1
        placed = wanted[:, None] & (position[:, None] == flat_places[None, :])
        packed_ids = jnp.sum(jnp.where(placed, held_slots[:, None], 0), axis=0)
        packed_owner = jnp.sum(jnp.where(placed, flat_owner[:, None], 0), axis=0)
        live_tiles = jnp.sum(wanted.astype(jnp.int32))

        def one_tile(tile_index, loop_state):
            query_grad, key_grads = loop_state
            key_block = packed_ids[tile_index]
            owner_block = packed_owner[tile_index]
            key_start = (
                key_block // (block_count * ka_count) * block_count + key_block % block_count
            ) * block_rows
            pair_tile = lax.dynamic_slice_in_dim(column_keys, key_start, block_rows, 0)
            key_tile = pair_tile[:, :head_width]
            value_tile = pair_tile[:, head_width:]
            query_tile = held_query.reshape(block_rows, part_heads, head_width)
            grad_tile = held_grad.reshape(block_rows, part_heads, head_width)
            scores = (
                jnp.einsum("rhd,cd->hrc", query_tile, key_tile, preferred_element_type=jnp.float32)
                * score_scale
            )
            query_pos = (first_block + owner_block) * block_rows + row_offsets
            key_pos = key_block * block_rows + row_offsets
            allowed = key_pos[None, :] <= query_pos[:, None]
            probs_full = jnp.exp(
                jnp.where(allowed[None], scores - total_rows[:, :, None], VERY_LOW)
            )
            prob_grads = jnp.einsum(
                "rhd,cd->hrc", grad_tile, value_tile, preferred_element_type=jnp.float32
            )
            score_grads = probs_full * (prob_grads - delta_rows[:, :, None])
            rounded_probs = probs_full.astype(jnp.bfloat16)
            rounded_grads = score_grads.astype(jnp.bfloat16)
            value_part = jnp.einsum(
                "hrc,rhd->cd", rounded_probs, grad_tile, preferred_element_type=jnp.float32
            )
            key_part = (
                jnp.einsum(
                    "hrc,rhd->cd", rounded_grads, query_tile, preferred_element_type=jnp.float32
                )
                * score_scale
            )
            query_part = (
                jnp.einsum(
                    "hrc,cd->rhd", rounded_grads, key_tile, preferred_element_type=jnp.float32
                )
                * score_scale
            )
            old_query = query_grad
            query_grad = old_query + query_part.reshape(block_rows, -1)
            old_keys = lax.dynamic_slice_in_dim(key_grads, key_start, block_rows, 0)
            key_grads = lax.dynamic_update_slice_in_dim(
                key_grads, old_keys + jnp.concatenate([key_part, value_part], 1), key_start, 0
            )
            return (query_grad, key_grads)

        return lax.fori_loop(0, live_tiles, one_tile, (query_grad, key_grads))

    query_part = query_rows
    grad_zero = jnp.zeros(query_part.shape, jnp.float32)
    row_stack = jnp.stack([query_part, out_grads, outputs])
    query_grad = grad_zero
    stat_stack = log_totals[None]

    def forward_hop(hop_index, loop_state):
        row_stack, query_grad, stat_stack, key_grads = loop_state
        anchor = (ka_index - hop_index) % ka_count
        query_grad, key_grads = visit_block(row_stack, query_grad, stat_stack, anchor, key_grads)
        row_stack = passed_along(row_stack, "ka", 1)
        query_grad, stat_stack = passed_along((query_grad, stat_stack), "ka", 1)
        return (row_stack, query_grad, stat_stack, key_grads)

    row_stack, query_grad, stat_stack, key_grads = lax.fori_loop(
        0, ka_count - 1, forward_hop, (row_stack, query_grad, stat_stack, key_grads)
    )
    query_grad, key_grads = visit_block(
        row_stack, query_grad, stat_stack, (ka_index + 1) % ka_count, key_grads
    )
    query_grad = passed_along(query_grad, "ka", 1)
    owned_grads = lax.psum_scatter(key_grads, "pb", scatter_dimension=0, tiled=True)
    return (query_grad, owned_grads[:, :head_width], owned_grads[:, head_width:])


MESH = pl.DeviceIdType.MESH
VMEM_BUDGET = 40 << 20


NT = (((1,), (1,)), ((), ()))
TN = (((0,), (0,)), ((), ()))
INFO = 128
INFO_C, INFO_P, KEY_P, KEY_C, VALUE_C, VALUE_P, KGRAD_P, KGRAD_C, VGRAD_C, VGRAD_P = range(10)


def tile_scores(key_tile, query_stack, total_row, scale):
    scores = lax.dot_general(key_tile, query_stack, NT, preferred_element_type=jnp.float32) * scale
    return scores - total_row


def tile_score_grads(probs, value_tile, grad_stack, delta_row):
    prob_grads = lax.dot_general(value_tile, grad_stack, NT, preferred_element_type=jnp.float32)
    return (probs * (prob_grads - delta_row)).astype(jnp.bfloat16)


def query_share(score_grads, key_tile, scale):
    return lax.dot_general(score_grads, key_tile, TN, preferred_element_type=jnp.float32) * scale


def whole_kernel(
    ka_count, inner, line_count,
    query_hbm, key_hbm, value_hbm, out_hbm, grad_hbm, total_hbm, selected_hbm, counts_hbm,
    query_grad_ref, key_grad_ref, value_grad_ref,
    query_ref, out_ref, grad_ref, total_ref, selected_ref, counts_ref,
    key_own, value_own, key_plane, value_column,
    key_picked, value_picked, key_in, value_in,
    key_part, value_part, kgrad_plane, vgrad_column,
    kgrad_sum, vgrad_sum, kgrad_matrix, vgrad_matrix, kgrad_in, vgrad_in,
    own_info, plane_info, column_info, query_stack, grad_stack, query_acc, key_acc, value_acc,
    send_sem, recv_sem, load_sem,
):
    bf, f32 = jnp.bfloat16, jnp.float32
    plane_count = inner * ka_count
    column_count = 2 * line_count
    pb_index, ka_index = lax.axis_index("pb"), lax.axis_index("ka")
    line = lax.div(pb_index, inner)
    row = lax.rem(pb_index, inner)
    place = row * ka_count + ka_index
    chip, core = lax.div(place, 2), lax.rem(place, 2)
    member = line * 2 + core
    block_rows, head_width = key_hbm.shape
    half_rows = block_rows // 2
    heads = total_hbm.shape[0]
    scale = head_width ** (-0.5)
    block = line * plane_count + place

    def half(which):
        if isinstance(which, int):
            return pl.ds(which * half_rows, half_rows)
        return pl.ds(pl.multiple_of(which * half_rows, half_rows), half_rows)

    def partner(me, offset, count):
        if count & (count - 1):
            return lax.rem(me + offset, count)
        peer, bit = me, 1
        while bit < count:
            if offset & bit:
                peer = peer + bit - 2 * bit * lax.rem(lax.div(me, bit), 2)
            bit *= 2
        return peer

    def plane_peer(offset):
        peer = partner(place, offset, plane_count)
        return peer, (line * inner + lax.div(peer, ka_count), lax.rem(peer, ka_count))

    def column_peer(offset):
        peer = partner(member, offset, column_count)
        there = chip * 2 + lax.rem(peer, 2)
        return peer, (lax.div(peer, 2) * inner + lax.div(there, ka_count), lax.rem(there, ka_count))

    plane = [plane_peer(offset) for offset in range(plane_count)]
    column = [column_peer(offset) for offset in range(column_count)]

    barrier = pltpu.get_barrier_semaphore()
    for group in (column, plane):
        for _, device in group[:0:-1]:
            pl.semaphore_signal(barrier, inc=1, device_id=device, device_id_type=MESH)
    loads = [
        pltpu.make_async_copy(source, target, load_sem.at[index])
        for index, (source, target) in enumerate((
            (selected_hbm, selected_ref), (counts_hbm, counts_ref),
            (key_hbm, key_own), (value_hbm, value_own),
            (key_hbm.at[half(core)], key_plane.at[place]), (value_hbm.at[half(core)], value_column.at[member]),
            (query_hbm, query_ref), (grad_hbm, grad_ref), (out_hbm, out_ref), (total_hbm, total_ref),
        ))
    ]
    for load in loads:
        load.start()

    loads[0].wait()
    loads[1].wait()
    target = jnp.where(counts_ref[0] > 1, selected_ref[0, 1], -1)
    own_info[0] = target
    plane_info[place, 0] = target
    column_info[member, 0] = target

    sent = []

    def send(leg, device, source, target):
        pltpu.make_async_remote_copy(
            src_ref=source, dst_ref=target, send_sem=send_sem.at[leg], recv_sem=recv_sem.at[leg],
            device_id=device, device_id_type=MESH,
        ).start()

    def whole_leg(leg, group, held):
        units = held.at[pl.ds(0, len(group) - 1)]
        return pltpu.make_async_remote_copy(
            src_ref=units, dst_ref=units, send_sem=send_sem.at[leg], recv_sem=recv_sem.at[leg],
            device_id=group[1][1], device_id_type=MESH,
        )

    def arrive(leg, group, held):
        whole_leg(leg, group, held).wait_recv()

    def settle():
        for started in sent:
            whole_leg(*started).wait_send()
        sent.clear()

    def farthest_first(group):
        return [(offset, *group[offset]) for offset in range(len(group) - 1, 0, -1)]

    for load in loads[2:6]:
        load.wait()
    pl.semaphore_wait(barrier, plane_count + column_count - 2)
    for _, _, device in farthest_first(column):
        send(INFO_C, device, own_info, column_info.at[member])
    for _, peer, device in farthest_first(column):
        send(VALUE_C, device, value_own.at[half(lax.rem(peer, 2))], value_column.at[member])
    for _, peer, device in farthest_first(plane):
        send(KEY_P, device, key_own.at[half(lax.rem(peer, 2))], key_plane.at[place])
    for _, _, device in farthest_first(plane):
        send(INFO_P, device, own_info, plane_info.at[place])
    sent += [(INFO_C, column, column_info), (VALUE_C, column, value_column)]
    sent += [(KEY_P, plane, key_plane), (INFO_P, plane, plane_info)]

    for load in loads[6:]:
        load.wait()
    deltas = []
    for head in range(heads):
        columns = pl.ds(head * head_width, head_width)
        rows = pl.ds(head * block_rows, block_rows)
        query_stack[rows, :] = query_ref[:, columns]
        grad_stack[rows, :] = grad_ref[:, columns]
        product = grad_ref[:, columns].astype(f32) * out_ref[:, columns].astype(f32)
        deltas.append(jnp.sum(product.T, axis=0, keepdims=True))
    delta_row = jnp.concatenate(deltas, axis=1)
    total_row = jnp.concatenate([total_ref[head : head + 1, :] for head in range(heads)], axis=1)
    stack_shape = (block_rows, heads * block_rows)
    key_offset = lax.broadcasted_iota(jnp.int32, stack_shape, 0)
    query_offset = lax.rem(lax.broadcasted_iota(jnp.int32, stack_shape, 1), block_rows)

    arrive(INFO_C, column, column_info)
    column_targets = [column_info[peer, 0] for peer, _ in column]
    arrive(KEY_P, plane, key_plane)
    for offset, _, device in farthest_first(column):
        key_picked[offset] = key_plane[lax.rem(jnp.maximum(column_targets[offset], 0), plane_count)]
        send(KEY_C, device, key_picked.at[offset], key_in.at[member])
    listed = jnp.maximum(target, 0)
    key_in[member] = key_plane[lax.rem(listed, plane_count)]

    arrive(INFO_P, plane, plane_info)
    plane_targets = [plane_info[peer, 0] for peer, _ in plane]
    arrive(VALUE_C, column, value_column)
    for offset, _, device in farthest_first(plane):
        wanted = jnp.maximum(plane_targets[offset], 0)
        value_picked[offset] = value_column[lax.div(wanted, plane_count) * 2 + lax.rem(wanted, 2)]
        send(VALUE_P, device, value_picked.at[offset], value_in.at[place])
    value_in[place] = value_column[lax.div(listed, plane_count) * 2 + lax.rem(listed, 2)]
    settle()
    sent += [(KEY_C, column, key_picked), (VALUE_P, plane, value_picked)]

    listed_total = jnp.where(target >= 0, total_row, -VERY_LOW)

    def owner_matrix(matrix, owners, targets):
        shape = (half_rows, len(targets) * half_rows)
        lane = lax.broadcasted_iota(jnp.int32, shape, 1)
        aimed = jnp.full(shape, targets[0], jnp.int32)
        for source in range(1, len(targets)):
            aimed = jnp.where(lane >= source * half_rows, targets[source], aimed)
        same_row = lax.rem(lane, half_rows) == lax.broadcasted_iota(jnp.int32, shape, 0)
        aimed = jnp.where(same_row, aimed, -1)
        for offset, owner in enumerate(owners):
            matrix[pl.ds(offset * half_rows, half_rows), :] = jnp.where(aimed == owner, 1.0, 0.0).astype(bf)

    owner_matrix(
        kgrad_matrix,
        [lax.div(peer, 2) * plane_count + chip * 2 + lax.rem(peer, 2) for peer, _ in column],
        [plane_info[source, 0] for source in range(plane_count)],
    )
    owner_matrix(
        vgrad_matrix,
        [line * plane_count + peer for peer, _ in plane],
        [column_info[source, 0] for source in range(column_count)],
    )
    own_key = key_own[...]
    scores = tile_scores(own_key, query_stack[...], total_row, scale)
    probs = jnp.exp(jnp.where(key_offset <= query_offset, scores, VERY_LOW))
    value_acc[...] = jnp.dot(probs.astype(bf), grad_stack[...], preferred_element_type=f32)
    score_grads = tile_score_grads(probs, value_own[...], grad_stack[...], delta_row)
    query_acc[...] = query_share(score_grads, own_key, scale)
    key_acc[...] = jnp.dot(score_grads, query_stack[...], preferred_element_type=f32) * scale

    def listed_tile(halves, pair):
        return jnp.concatenate([halves[2 * pair], halves[2 * pair + 1]], axis=0)

    arrive(KEY_C, column, key_in)
    key_tile = listed_tile(key_in, lax.div(listed, plane_count))
    probs = jnp.exp(tile_scores(key_tile, query_stack[...], listed_total, scale))
    value_part[...] = jnp.dot(probs.astype(bf), grad_stack[...], preferred_element_type=f32).astype(bf)
    for _, peer, device in farthest_first(column):
        send(VGRAD_C, device, value_part.at[half(lax.rem(peer, 2))], vgrad_column.at[member])
    vgrad_column[member] = value_part[half(core), :]
    arrive(VALUE_P, plane, value_in)
    value_tile = listed_tile(value_in, lax.div(lax.rem(listed, plane_count), 2))
    score_grads = tile_score_grads(probs, value_tile, grad_stack[...], delta_row)
    key_part[...] = (jnp.dot(score_grads, query_stack[...], preferred_element_type=f32) * scale).astype(bf)
    for _, peer, device in farthest_first(plane):
        send(KGRAD_P, device, key_part.at[half(lax.rem(peer, 2))], kgrad_plane.at[place])
    kgrad_plane[place] = key_part[half(core), :]
    settle()
    sent += [(VGRAD_C, column, vgrad_column), (KGRAD_P, plane, kgrad_plane)]
    query_acc[...] += query_share(score_grads, key_tile, scale)
    for head in range(heads):
        query_grad_ref[:, pl.ds(head * head_width, head_width)] = query_acc[
            pl.ds(head * block_rows, block_rows), :
        ]

    def owner_sums(matrix, held):
        rows = held.shape[0] * half_rows
        return jnp.dot(matrix[...], held[...].reshape(rows, head_width), preferred_element_type=f32).astype(bf)

    arrive(KGRAD_P, plane, kgrad_plane)
    kgrad_sum[...] = owner_sums(kgrad_matrix, kgrad_plane).reshape(kgrad_sum.shape)
    for offset, _, device in farthest_first(column):
        send(KGRAD_C, device, kgrad_sum.at[offset], kgrad_in.at[member])
    kgrad_in[member] = kgrad_sum[0]

    arrive(VGRAD_C, column, vgrad_column)
    vgrad_sum[...] = owner_sums(vgrad_matrix, vgrad_column).reshape(vgrad_sum.shape)
    for offset, _, device in farthest_first(plane):
        send(VGRAD_P, device, vgrad_sum.at[offset], vgrad_in.at[place])
    vgrad_in[place] = vgrad_sum[0]
    sent += [(KGRAD_C, column, kgrad_sum), (VGRAD_P, plane, vgrad_sum)]
    settle()

    def grown(total, halves):
        parts = halves[...].astype(f32).reshape(halves.shape[0] // 2, block_rows, head_width)
        return total + jnp.sum(parts, axis=0)

    arrive(KGRAD_C, column, kgrad_in)
    key_grad_ref[...] = grown(key_acc[...], kgrad_in)
    arrive(VGRAD_P, plane, vgrad_in)
    value_grad_ref[...] = grown(value_acc[...], vgrad_in)


def kernel_shards(query_rows, key_rows, value_rows, outputs, out_grads, log_totals, selected, counts):
    ka_count, pb_count = lax.axis_size("ka"), lax.axis_size("pb")
    inner = 2 if pb_count % 2 == 0 else 1
    line_count, plane_count = pb_count // inner, inner * ka_count
    column_count = 2 * line_count
    block_rows, head_width = key_rows.shape
    heads = log_totals.shape[0]
    tile = key_rows.shape
    half_rows = block_rows // 2
    part = (half_rows, head_width)
    dma = pltpu.SemaphoreType.DMA
    vmem = pl.BlockSpec(memory_space=pltpu.VMEM)
    hbm = pl.BlockSpec(memory_space=pl.ANY)
    bf, f32 = jnp.bfloat16, jnp.float32
    shapes = (query_rows.shape, key_rows.shape, value_rows.shape)
    held = pl.pallas_call(
        functools.partial(whole_kernel, ka_count, inner, line_count),
        out_shape=tuple(pltpu.VMEM(shape, f32) for shape in shapes),
        in_specs=[hbm] * 8,
        out_specs=(vmem, vmem, vmem),
        scratch_shapes=[
            pltpu.VMEM(query_rows.shape, bf),
            pltpu.VMEM(query_rows.shape, bf),
            pltpu.VMEM(query_rows.shape, bf),
            pltpu.VMEM(log_totals.shape, f32),
            pltpu.SMEM(selected.shape, jnp.int32),
            pltpu.SMEM(counts.shape, jnp.int32),
            pltpu.VMEM(tile, bf),
            pltpu.VMEM(tile, bf),
            pltpu.VMEM((plane_count, *part), bf),
            pltpu.VMEM((column_count, *part), bf),
            pltpu.VMEM((column_count, *part), bf),
            pltpu.VMEM((plane_count, *part), bf),
            pltpu.VMEM((column_count, *part), bf),
            pltpu.VMEM((plane_count, *part), bf),
            pltpu.VMEM(tile, bf),
            pltpu.VMEM(tile, bf),
            pltpu.VMEM((plane_count, *part), bf),
            pltpu.VMEM((column_count, *part), bf),
            pltpu.VMEM((column_count, *part), bf),
            pltpu.VMEM((plane_count, *part), bf),
            pltpu.VMEM((column_count * half_rows, plane_count * half_rows), bf),
            pltpu.VMEM((plane_count * half_rows, column_count * half_rows), bf),
            pltpu.VMEM((column_count, *part), bf),
            pltpu.VMEM((plane_count, *part), bf),
            pltpu.SMEM((INFO,), jnp.int32),
            pltpu.SMEM((plane_count, INFO), jnp.int32),
            pltpu.SMEM((column_count, INFO), jnp.int32),
            pltpu.VMEM((heads * block_rows, head_width), bf),
            pltpu.VMEM((heads * block_rows, head_width), bf),
            pltpu.VMEM((heads * block_rows, head_width), f32),
            pltpu.VMEM(tile, f32),
            pltpu.VMEM(tile, f32),
            dma((10,)),
            dma((10,)),
            dma((10,)),
        ],
        compiler_params=pltpu.CompilerParams(collective_id=0, has_side_effects=True),
    )(query_rows, key_rows, value_rows, outputs, out_grads, log_totals, selected, counts)
    return pl.pallas_call(
        write_kernel,
        out_shape=tuple(jax.ShapeDtypeStruct(shape, f32) for shape in shapes),
        in_specs=[vmem] * 3,
        out_specs=(hbm, hbm, hbm),
        scratch_shapes=[dma((3,))],
    )(*[pltpu.with_memory_space_constraint(part, pltpu.VMEM) for part in held])


def write_kernel(*refs):
    sources, targets, sem = refs[:3], refs[3:6], refs[6]
    stores = [pltpu.make_async_copy(*pair, sem.at[i]) for i, pair in enumerate(zip(sources, targets))]
    for store in stores:
        store.start()
    for store in stores:
        store.wait()


def fits_kernel(query_rows, key_rows, value_rows, outputs, out_grads, log_totals, selected, counts):
    pb_count, ka_count = lax.axis_size("pb"), lax.axis_size("ka")
    block_rows, head_width = key_rows.shape
    inner = 2 if pb_count % 2 == 0 else 1
    tile_bytes = 2 * block_rows * head_width
    tiles = 6 * (pb_count // inner + inner * ka_count)
    return (
        selected.shape[0] == 1
        and selected.shape[1] == 2
        and ka_count % 2 == 0
        and pb_count > inner
        and block_rows == head_width == 128
        and tiles * tile_bytes < VMEM_BUDGET
    )


def either(*arrays):
    return kernel_shards(*arrays) if fits_kernel(*arrays) else shards(*arrays)


def solution(mesh):
    return jax.shard_map(
        either,
        mesh=mesh,
        in_specs=(
            P(("pb", "ka"), None),
            P(("pb", "ka"), None),
            P(("pb", "ka"), None),
            P(("pb", "ka"), None),
            P(("pb", "ka"), None),
            P(None, ("pb", "ka")),
            P(("pb", "ka"), None),
            P(("pb", "ka")),
        ),
        out_specs=(P(("pb", "ka"), None), P(("pb", "ka"), None), P(("pb", "ka"), None)),
        check_vma=False,
    )
```

```python
import functools

import jax
import jax.numpy as jnp
from jax import lax
from jax.experimental import pallas as pl
from jax.experimental.pallas import tpu as pltpu
from jax.sharding import PartitionSpec as P

VERY_LOW = -1e30


def passed_along(value, axis, steps):
    count = lax.axis_size(axis)
    pairs = [(source, (source + steps) % count) for source in range(count)]
    return lax.ppermute(value, axis, pairs)


def head_sums(grad_rows, out_rows, head_width):
    row_total = grad_rows.shape[0]
    part_heads = grad_rows.shape[1] // head_width
    product = grad_rows.astype(jnp.float32) * out_rows.astype(jnp.float32)
    return jnp.sum(product.reshape(row_total, part_heads, head_width), axis=2).T


def shards(query_rows, key_rows, value_rows, outputs, out_grads, log_totals, selected, counts):
    ka_count = lax.axis_size("ka")
    ka_index = lax.axis_index("ka")
    pb_index = lax.axis_index("pb")
    block_count = selected.shape[0]
    slot_count = selected.shape[1]
    head_width = key_rows.shape[1]
    block_rows = query_rows.shape[0] // block_count
    score_scale = head_width ** (-0.5)
    key_pairs = jnp.concatenate([key_rows, value_rows], 1)
    column_keys = lax.all_gather(key_pairs, "pb", axis=0, tiled=True)
    peer_slots, peer_counts = (
        lax.all_gather(selected, "ka", axis=0, tiled=True),
        lax.all_gather(counts, "ka", axis=0, tiled=True),
    )
    key_grads = jnp.zeros((column_keys.shape[0], 2 * head_width), jnp.float32)
    row_offsets = jnp.arange(block_rows, dtype=jnp.int32)
    flat_owner = jnp.repeat(jnp.arange(block_count, dtype=jnp.int32), slot_count)
    flat_slot = jnp.tile(jnp.arange(slot_count, dtype=jnp.int32), block_count)
    flat_places = jnp.arange(block_count * slot_count, dtype=jnp.int32)

    def visit_block(row_stack, query_grad, stat_stack, anchor, key_grads):
        held_query = row_stack[0]
        held_grad = row_stack[1]
        total_rows = stat_stack[0]
        delta_rows = head_sums(row_stack[1], row_stack[2], head_width)
        part_heads = total_rows.shape[0]
        held_slots = lax.dynamic_slice_in_dim(
            peer_slots, anchor * block_count, block_count, 0
        ).reshape(-1)
        held_counts = jnp.repeat(
            lax.dynamic_slice_in_dim(peer_counts, anchor * block_count, block_count, 0), slot_count
        )
        first_block = (pb_index * ka_count + anchor) * block_count
        wanted = (flat_slot < held_counts) & (held_slots // block_count % ka_count == ka_index)
        earlier = flat_places[None, :] <= flat_places[:, None]
        position = jnp.sum((earlier & wanted[None, :]).astype(jnp.int32), axis=1) - 1
        placed = wanted[:, None] & (position[:, None] == flat_places[None, :])
        packed_ids = jnp.sum(jnp.where(placed, held_slots[:, None], 0), axis=0)
        packed_owner = jnp.sum(jnp.where(placed, flat_owner[:, None], 0), axis=0)
        live_tiles = jnp.sum(wanted.astype(jnp.int32))

        def one_tile(tile_index, loop_state):
            query_grad, key_grads = loop_state
            key_block = packed_ids[tile_index]
            owner_block = packed_owner[tile_index]
            key_start = (
                key_block // (block_count * ka_count) * block_count + key_block % block_count
            ) * block_rows
            pair_tile = lax.dynamic_slice_in_dim(column_keys, key_start, block_rows, 0)
            key_tile = pair_tile[:, :head_width]
            value_tile = pair_tile[:, head_width:]
            query_tile = held_query.reshape(block_rows, part_heads, head_width)
            grad_tile = held_grad.reshape(block_rows, part_heads, head_width)
            scores = (
                jnp.einsum("rhd,cd->hrc", query_tile, key_tile, preferred_element_type=jnp.float32)
                * score_scale
            )
            query_pos = (first_block + owner_block) * block_rows + row_offsets
            key_pos = key_block * block_rows + row_offsets
            allowed = key_pos[None, :] <= query_pos[:, None]
            probs_full = jnp.exp(
                jnp.where(allowed[None], scores - total_rows[:, :, None], VERY_LOW)
            )
            prob_grads = jnp.einsum(
                "rhd,cd->hrc", grad_tile, value_tile, preferred_element_type=jnp.float32
            )
            score_grads = probs_full * (prob_grads - delta_rows[:, :, None])
            rounded_probs = probs_full.astype(jnp.bfloat16)
            rounded_grads = score_grads.astype(jnp.bfloat16)
            value_part = jnp.einsum(
                "hrc,rhd->cd", rounded_probs, grad_tile, preferred_element_type=jnp.float32
            )
            key_part = (
                jnp.einsum(
                    "hrc,rhd->cd", rounded_grads, query_tile, preferred_element_type=jnp.float32
                )
                * score_scale
            )
            query_part = (
                jnp.einsum(
                    "hrc,cd->rhd", rounded_grads, key_tile, preferred_element_type=jnp.float32
                )
                * score_scale
            )
            old_query = query_grad
            query_grad = old_query + query_part.reshape(block_rows, -1)
            old_keys = lax.dynamic_slice_in_dim(key_grads, key_start, block_rows, 0)
            key_grads = lax.dynamic_update_slice_in_dim(
                key_grads, old_keys + jnp.concatenate([key_part, value_part], 1), key_start, 0
            )
            return (query_grad, key_grads)

        return lax.fori_loop(0, live_tiles, one_tile, (query_grad, key_grads))

    query_part = query_rows
    grad_zero = jnp.zeros(query_part.shape, jnp.float32)
    row_stack = jnp.stack([query_part, out_grads, outputs])
    query_grad = grad_zero
    stat_stack = log_totals[None]

    def forward_hop(hop_index, loop_state):
        row_stack, query_grad, stat_stack, key_grads = loop_state
        anchor = (ka_index - hop_index) % ka_count
        query_grad, key_grads = visit_block(row_stack, query_grad, stat_stack, anchor, key_grads)
        row_stack = passed_along(row_stack, "ka", 1)
        query_grad, stat_stack = passed_along((query_grad, stat_stack), "ka", 1)
        return (row_stack, query_grad, stat_stack, key_grads)

    row_stack, query_grad, stat_stack, key_grads = lax.fori_loop(
        0, ka_count - 1, forward_hop, (row_stack, query_grad, stat_stack, key_grads)
    )
    query_grad, key_grads = visit_block(
        row_stack, query_grad, stat_stack, (ka_index + 1) % ka_count, key_grads
    )
    query_grad = passed_along(query_grad, "ka", 1)
    owned_grads = lax.psum_scatter(key_grads, "pb", scatter_dimension=0, tiled=True)
    return (query_grad, owned_grads[:, :head_width], owned_grads[:, head_width:])


MESH = pl.DeviceIdType.MESH
VMEM_BUDGET = 40 << 20


NT = (((1,), (1,)), ((), ()))
TN = (((0,), (0,)), ((), ()))
INFO = 128
INFO_C, INFO_P, KEY_P, KEY_C, VALUE_C, VALUE_P, KGRAD_P, KGRAD_C, VGRAD_C, VGRAD_P = range(10)


def tile_scores(key_tile, query_stack, total_row, scale):
    scores = lax.dot_general(key_tile, query_stack, NT, preferred_element_type=jnp.float32) * scale
    return scores - total_row


def tile_score_grads(probs, value_tile, grad_stack, delta_row):
    prob_grads = lax.dot_general(value_tile, grad_stack, NT, preferred_element_type=jnp.float32)
    return (probs * (prob_grads - delta_row)).astype(jnp.bfloat16)


def query_share(score_grads, key_tile, scale):
    return lax.dot_general(score_grads, key_tile, TN, preferred_element_type=jnp.float32) * scale


def whole_kernel(
    ka_count, inner, line_count,
    query_hbm, key_hbm, value_hbm, out_hbm, grad_hbm, total_hbm, selected_hbm, counts_hbm,
    query_grad_ref, key_grad_ref, value_grad_ref,
    query_ref, out_ref, grad_ref, total_ref, selected_ref, counts_ref,
    key_own, value_own, key_plane, value_column,
    key_picked, value_picked, key_in, value_in,
    key_part, value_part, kgrad_plane, vgrad_column,
    kgrad_sum, vgrad_sum, kgrad_matrix, vgrad_matrix, kgrad_in, vgrad_in,
    own_info, plane_info, column_info, query_stack, grad_stack, query_acc, key_acc, value_acc,
    send_sem, recv_sem, load_sem,
):
    bf, f32 = jnp.bfloat16, jnp.float32
    plane_count = inner * ka_count
    column_count = 2 * line_count
    pb_index, ka_index = lax.axis_index("pb"), lax.axis_index("ka")
    line = lax.div(pb_index, inner)
    row = lax.rem(pb_index, inner)
    place = row * ka_count + ka_index
    chip, core = lax.div(place, 2), lax.rem(place, 2)
    member = line * 2 + core
    block_rows, head_width = key_hbm.shape
    half_rows = block_rows // 2
    heads = total_hbm.shape[0]
    scale = head_width ** (-0.5)
    block = line * plane_count + place

    def half(which):
        if isinstance(which, int):
            return pl.ds(which * half_rows, half_rows)
        return pl.ds(pl.multiple_of(which * half_rows, half_rows), half_rows)

    def others(me, count):
        return [other + lax.convert_element_type(other >= me, jnp.int32) for other in range(count - 1)]

    def plane_of(places):
        return [
            (peer, (line * inner + lax.div(peer, ka_count), lax.rem(peer, ka_count)))
            for peer in [place, *places]
        ]

    def column_of(lines):
        peers = [member, line * 2 + 1 - core]
        for other in lines:
            peers += [other * 2 + 1 - core, other * 2 + core]
        return [
            (peer, (
                lax.div(peer, 2) * inner + lax.div(chip * 2 + lax.rem(peer, 2), ka_count),
                lax.rem(chip * 2 + lax.rem(peer, 2), ka_count),
            ))
            for peer in peers
        ]

    rising = others(line, line_count)
    places = others(place, plane_count)
    plane = plane_of(places)
    plane_back = plane_of(places[::-1])
    column = column_of(rising)
    column_back = column_of(rising[::-1])

    barrier = pltpu.get_barrier_semaphore()
    for group in (column, plane):
        for _, device in group[:0:-1]:
            pl.semaphore_signal(barrier, inc=1, device_id=device, device_id_type=MESH)
    loads = [
        pltpu.make_async_copy(source, target, load_sem.at[index])
        for index, (source, target) in enumerate((
            (selected_hbm, selected_ref), (counts_hbm, counts_ref),
            (key_hbm, key_own), (value_hbm, value_own),
            (query_hbm, query_ref), (grad_hbm, grad_ref), (out_hbm, out_ref), (total_hbm, total_ref),
        ))
    ]
    for load in loads:
        load.start()

    loads[0].wait()
    loads[1].wait()
    target = jnp.where(counts_ref[0] > 1, selected_ref[0, 1], -1)
    own_line = jnp.full(own_info.shape, target, jnp.int32)
    own_info[...] = own_line
    plane_info[place] = own_line
    column_info[member] = own_line

    sent = []

    def send(leg, device, source, target):
        pltpu.make_async_remote_copy(
            src_ref=source, dst_ref=target, send_sem=send_sem.at[leg], recv_sem=recv_sem.at[leg],
            device_id=device, device_id_type=MESH,
        ).start()

    def whole_leg(leg, group, held):
        units = held.at[pl.ds(0, len(group) - 1)]
        return pltpu.make_async_remote_copy(
            src_ref=units, dst_ref=units, send_sem=send_sem.at[leg], recv_sem=recv_sem.at[leg],
            device_id=group[1][1], device_id_type=MESH,
        )

    def arrive(leg, group, held):
        whole_leg(leg, group, held).wait_recv()

    def settle():
        for started in sent:
            whole_leg(*started).wait_send()
        sent.clear()

    def farthest_first(group):
        return [(offset, *group[offset]) for offset in range(len(group) - 1, 0, -1)]

    for load in loads[2:4]:
        load.wait()
    key_plane[place] = key_own[half(core), :]
    value_column[member] = value_own[half(core), :]
    pl.semaphore_wait(barrier, plane_count + column_count - 2)
    for _, _, device in farthest_first(column):
        send(INFO_C, device, own_info, column_info.at[member])
    for _, peer, device in farthest_first(column):
        send(VALUE_C, device, value_own.at[half(lax.rem(peer, 2))], value_column.at[member])
    for _, peer, device in farthest_first(plane):
        send(KEY_P, device, key_own.at[half(lax.rem(peer, 2))], key_plane.at[place])
    for _, _, device in farthest_first(plane):
        send(INFO_P, device, own_info, plane_info.at[place])
    sent += [(INFO_C, column, column_info), (VALUE_C, column, value_column)]
    sent += [(KEY_P, plane, key_plane), (INFO_P, plane, plane_info)]

    for load in loads[4:]:
        load.wait()
    deltas = []
    for head in range(heads):
        columns = pl.ds(head * head_width, head_width)
        rows = pl.ds(head * block_rows, block_rows)
        query_stack[rows, :] = query_ref[:, columns]
        grad_stack[rows, :] = grad_ref[:, columns]
        product = grad_ref[:, columns].astype(f32) * out_ref[:, columns].astype(f32)
        deltas.append(jnp.sum(product.T, axis=0, keepdims=True))
    delta_row = jnp.concatenate(deltas, axis=1)
    total_row = jnp.concatenate([total_ref[head : head + 1, :] for head in range(heads)], axis=1)
    stack_shape = (block_rows, heads * block_rows)
    key_offset = lax.broadcasted_iota(jnp.int32, stack_shape, 0)
    query_offset = lax.rem(lax.broadcasted_iota(jnp.int32, stack_shape, 1), block_rows)

    arrive(INFO_C, column, column_info)
    column_targets = [column_info[peer][0, 0] for peer, _ in column]
    arrive(KEY_P, plane, key_plane)
    for offset, _, device in farthest_first(column):
        key_picked[offset] = key_plane[lax.rem(jnp.maximum(column_targets[offset], 0), plane_count)]
        send(KEY_C, device, key_picked.at[offset], key_in.at[member])
    listed = jnp.maximum(target, 0)
    key_in[member] = key_plane[lax.rem(listed, plane_count)]

    arrive(INFO_P, plane, plane_info)
    plane_targets = [plane_info[peer][0, 0] for peer, _ in plane]
    arrive(VALUE_C, column, value_column)
    for offset, _, device in farthest_first(plane):
        wanted = jnp.maximum(plane_targets[offset], 0)
        value_picked[offset] = value_column[lax.div(wanted, plane_count) * 2 + lax.rem(wanted, 2)]
        send(VALUE_P, device, value_picked.at[offset], value_in.at[place])
    value_in[place] = value_column[lax.div(listed, plane_count) * 2 + lax.rem(listed, 2)]
    settle()
    sent += [(KEY_C, column, key_picked), (VALUE_P, plane, value_picked)]

    listed_total = jnp.where(target >= 0, total_row, -VERY_LOW)

    def owner_matrix(matrix, owners, targets):
        shape = (half_rows, len(targets) * half_rows)
        lane = lax.broadcasted_iota(jnp.int32, shape, 1)
        aimed = jnp.full(shape, targets[0], jnp.int32)
        for source in range(1, len(targets)):
            aimed = jnp.where(lane >= source * half_rows, targets[source], aimed)
        same_row = lax.rem(lane, half_rows) == lax.broadcasted_iota(jnp.int32, shape, 0)
        aimed = jnp.where(same_row, aimed, -1)
        for offset, owner in enumerate(owners):
            matrix[pl.ds(offset * half_rows, half_rows), :] = jnp.where(aimed == owner, 1.0, 0.0).astype(bf)

    owner_matrix(
        kgrad_matrix,
        [lax.div(peer, 2) * plane_count + chip * 2 + lax.rem(peer, 2) for peer, _ in column_back],
        [plane_info[source][0, 0] for source in range(plane_count)],
    )
    owner_matrix(
        vgrad_matrix,
        [line * plane_count + peer for peer, _ in plane_back],
        [column_info[source][0, 0] for source in range(column_count)],
    )
    own_key = key_own[...]
    scores = tile_scores(own_key, query_stack[...], total_row, scale)
    probs = jnp.exp(jnp.where(key_offset <= query_offset, scores, VERY_LOW))
    value_acc[...] = jnp.dot(probs.astype(bf), grad_stack[...], preferred_element_type=f32)
    score_grads = tile_score_grads(probs, value_own[...], grad_stack[...], delta_row)
    query_acc[...] = query_share(score_grads, own_key, scale)
    key_acc[...] = jnp.dot(score_grads, query_stack[...], preferred_element_type=f32) * scale

    def listed_tile(halves, pair):
        return jnp.concatenate([halves[2 * pair], halves[2 * pair + 1]], axis=0)

    arrive(VALUE_P, plane, value_in)
    value_tile = listed_tile(value_in, lax.div(lax.rem(listed, plane_count), 2))
    prob_grads = lax.dot_general(value_tile, grad_stack[...], NT, preferred_element_type=f32) - delta_row
    arrive(KEY_C, column, key_in)
    key_tile = listed_tile(key_in, lax.div(listed, plane_count))
    probs = jnp.exp(tile_scores(key_tile, query_stack[...], listed_total, scale))
    value_part[...] = jnp.dot(probs.astype(bf), grad_stack[...], preferred_element_type=f32).astype(bf)
    score_grads = (probs * prob_grads).astype(bf)
    key_part[...] = (jnp.dot(score_grads, query_stack[...], preferred_element_type=f32) * scale).astype(bf)
    for _, peer, device in farthest_first(column_back):
        send(VGRAD_C, device, value_part.at[half(lax.rem(peer, 2))], vgrad_column.at[member])
    for _, peer, device in farthest_first(plane_back):
        send(KGRAD_P, device, key_part.at[half(lax.rem(peer, 2))], kgrad_plane.at[place])
    vgrad_column[member] = value_part[half(core), :]
    kgrad_plane[place] = key_part[half(core), :]
    settle()
    sent += [(VGRAD_C, column, vgrad_column), (KGRAD_P, plane, kgrad_plane)]
    query_acc[...] += query_share(score_grads, key_tile, scale)
    for head in range(heads):
        query_grad_ref[:, pl.ds(head * head_width, head_width)] = query_acc[
            pl.ds(head * block_rows, block_rows), :
        ]

    def owner_sums(matrix, held):
        rows = held.shape[0] * half_rows
        return jnp.dot(matrix[...], held[...].reshape(rows, head_width), preferred_element_type=f32).astype(bf)

    arrive(KGRAD_P, plane, kgrad_plane)
    kgrad_sum[...] = owner_sums(kgrad_matrix, kgrad_plane).reshape(kgrad_sum.shape)
    for offset, _, device in farthest_first(column_back):
        send(KGRAD_C, device, kgrad_sum.at[offset], kgrad_in.at[member])
    kgrad_in[member] = kgrad_sum[0]

    arrive(VGRAD_C, column, vgrad_column)
    vgrad_sum[...] = owner_sums(vgrad_matrix, vgrad_column).reshape(vgrad_sum.shape)
    for offset, _, device in farthest_first(plane_back):
        send(VGRAD_P, device, vgrad_sum.at[offset], vgrad_in.at[place])
    vgrad_in[place] = vgrad_sum[0]
    sent += [(KGRAD_C, column, kgrad_sum), (VGRAD_P, plane, vgrad_sum)]
    settle()

    def grown(total, halves):
        parts = halves[...].astype(f32).reshape(halves.shape[0] // 2, block_rows, head_width)
        return total + jnp.sum(parts, axis=0)

    arrive(KGRAD_C, column, kgrad_in)
    key_grad_ref[...] = grown(key_acc[...], kgrad_in)
    arrive(VGRAD_P, plane, vgrad_in)
    value_grad_ref[...] = grown(value_acc[...], vgrad_in)


def kernel_shards(query_rows, key_rows, value_rows, outputs, out_grads, log_totals, selected, counts):
    ka_count, pb_count = lax.axis_size("ka"), lax.axis_size("pb")
    inner = 2 if pb_count % 2 == 0 else 1
    line_count, plane_count = pb_count // inner, inner * ka_count
    column_count = 2 * line_count
    block_rows, head_width = key_rows.shape
    heads = log_totals.shape[0]
    tile = key_rows.shape
    half_rows = block_rows // 2
    part = (half_rows, head_width)
    dma = pltpu.SemaphoreType.DMA
    vmem = pl.BlockSpec(memory_space=pltpu.VMEM)
    hbm = pl.BlockSpec(memory_space=pl.ANY)
    bf, f32 = jnp.bfloat16, jnp.float32
    shapes = (query_rows.shape, key_rows.shape, value_rows.shape)
    held = pl.pallas_call(
        functools.partial(whole_kernel, ka_count, inner, line_count),
        out_shape=tuple(pltpu.VMEM(shape, f32) for shape in shapes),
        in_specs=[hbm] * 8,
        out_specs=(vmem, vmem, vmem),
        scratch_shapes=[
            pltpu.VMEM(query_rows.shape, bf),
            pltpu.VMEM(query_rows.shape, bf),
            pltpu.VMEM(query_rows.shape, bf),
            pltpu.VMEM(log_totals.shape, f32),
            pltpu.SMEM(selected.shape, jnp.int32),
            pltpu.SMEM(counts.shape, jnp.int32),
            pltpu.VMEM(tile, bf),
            pltpu.VMEM(tile, bf),
            pltpu.VMEM((plane_count, *part), bf),
            pltpu.VMEM((column_count, *part), bf),
            pltpu.VMEM((column_count, *part), bf),
            pltpu.VMEM((plane_count, *part), bf),
            pltpu.VMEM((column_count, *part), bf),
            pltpu.VMEM((plane_count, *part), bf),
            pltpu.VMEM(tile, bf),
            pltpu.VMEM(tile, bf),
            pltpu.VMEM((plane_count, *part), bf),
            pltpu.VMEM((column_count, *part), bf),
            pltpu.VMEM((column_count, *part), bf),
            pltpu.VMEM((plane_count, *part), bf),
            pltpu.VMEM((column_count * half_rows, plane_count * half_rows), bf),
            pltpu.VMEM((plane_count * half_rows, column_count * half_rows), bf),
            pltpu.VMEM((column_count, *part), bf),
            pltpu.VMEM((plane_count, *part), bf),
            pltpu.VMEM((1, INFO), jnp.int32),
            pltpu.VMEM((plane_count, 1, INFO), jnp.int32),
            pltpu.VMEM((column_count, 1, INFO), jnp.int32),
            pltpu.VMEM((heads * block_rows, head_width), bf),
            pltpu.VMEM((heads * block_rows, head_width), bf),
            pltpu.VMEM((heads * block_rows, head_width), f32),
            pltpu.VMEM(tile, f32),
            pltpu.VMEM(tile, f32),
            dma((10,)),
            dma((10,)),
            dma((8,)),
        ],
        compiler_params=pltpu.CompilerParams(collective_id=0, has_side_effects=True),
    )(query_rows, key_rows, value_rows, outputs, out_grads, log_totals, selected, counts)
    return pl.pallas_call(
        write_kernel,
        out_shape=tuple(jax.ShapeDtypeStruct(shape, f32) for shape in shapes),
        in_specs=[vmem] * 3,
        out_specs=(hbm, hbm, hbm),
        scratch_shapes=[dma((3,))],
    )(*[pltpu.with_memory_space_constraint(part, pltpu.VMEM) for part in held])


def write_kernel(*refs):
    sources, targets, sem = refs[:3], refs[3:6], refs[6]
    stores = [pltpu.make_async_copy(*pair, sem.at[i]) for i, pair in enumerate(zip(sources, targets))]
    for store in stores:
        store.start()
    for store in stores:
        store.wait()


def fits_kernel(query_rows, key_rows, value_rows, outputs, out_grads, log_totals, selected, counts):
    pb_count, ka_count = lax.axis_size("pb"), lax.axis_size("ka")
    block_rows, head_width = key_rows.shape
    inner = 2 if pb_count % 2 == 0 else 1
    tile_bytes = 2 * block_rows * head_width
    tiles = 6 * (pb_count // inner + inner * ka_count)
    return (
        selected.shape[0] == 1
        and selected.shape[1] == 2
        and ka_count % 2 == 0
        and pb_count > inner
        and block_rows == head_width == 128
        and tiles * tile_bytes < VMEM_BUDGET
    )


def either(*arrays):
    return kernel_shards(*arrays) if fits_kernel(*arrays) else shards(*arrays)


def solution(mesh):
    return jax.shard_map(
        either,
        mesh=mesh,
        in_specs=(
            P(("pb", "ka"), None),
            P(("pb", "ka"), None),
            P(("pb", "ka"), None),
            P(("pb", "ka"), None),
            P(("pb", "ka"), None),
            P(None, ("pb", "ka")),
            P(("pb", "ka"), None),
            P(("pb", "ka")),
        ),
        out_specs=(P(("pb", "ka"), None), P(("pb", "ka"), None), P(("pb", "ka"), None)),
        check_vma=False,
    )
```

```python
import functools

import jax
import jax.numpy as jnp
from jax import lax
from jax.experimental import pallas as pl
from jax.experimental.pallas import tpu as pltpu
from jax.sharding import PartitionSpec as P

VERY_LOW = -1e30


def passed_along(value, axis, steps):
    count = lax.axis_size(axis)
    pairs = [(source, (source + steps) % count) for source in range(count)]
    return lax.ppermute(value, axis, pairs)


def head_sums(grad_rows, out_rows, head_width):
    row_total = grad_rows.shape[0]
    part_heads = grad_rows.shape[1] // head_width
    product = grad_rows.astype(jnp.float32) * out_rows.astype(jnp.float32)
    return jnp.sum(product.reshape(row_total, part_heads, head_width), axis=2).T


def shards(query_rows, key_rows, value_rows, outputs, out_grads, log_totals, selected, counts):
    ka_count = lax.axis_size("ka")
    ka_index = lax.axis_index("ka")
    pb_index = lax.axis_index("pb")
    block_count = selected.shape[0]
    slot_count = selected.shape[1]
    head_width = key_rows.shape[1]
    block_rows = query_rows.shape[0] // block_count
    score_scale = head_width ** (-0.5)
    key_pairs = jnp.concatenate([key_rows, value_rows], 1)
    column_keys = lax.all_gather(key_pairs, "pb", axis=0, tiled=True)
    peer_slots, peer_counts = (
        lax.all_gather(selected, "ka", axis=0, tiled=True),
        lax.all_gather(counts, "ka", axis=0, tiled=True),
    )
    key_grads = jnp.zeros((column_keys.shape[0], 2 * head_width), jnp.float32)
    row_offsets = jnp.arange(block_rows, dtype=jnp.int32)
    flat_owner = jnp.repeat(jnp.arange(block_count, dtype=jnp.int32), slot_count)
    flat_slot = jnp.tile(jnp.arange(slot_count, dtype=jnp.int32), block_count)
    flat_places = jnp.arange(block_count * slot_count, dtype=jnp.int32)

    def visit_block(row_stack, query_grad, stat_stack, anchor, key_grads):
        held_query = row_stack[0]
        held_grad = row_stack[1]
        total_rows = stat_stack[0]
        delta_rows = head_sums(row_stack[1], row_stack[2], head_width)
        part_heads = total_rows.shape[0]
        held_slots = lax.dynamic_slice_in_dim(
            peer_slots, anchor * block_count, block_count, 0
        ).reshape(-1)
        held_counts = jnp.repeat(
            lax.dynamic_slice_in_dim(peer_counts, anchor * block_count, block_count, 0), slot_count
        )
        first_block = (pb_index * ka_count + anchor) * block_count
        wanted = (flat_slot < held_counts) & (held_slots // block_count % ka_count == ka_index)
        earlier = flat_places[None, :] <= flat_places[:, None]
        position = jnp.sum((earlier & wanted[None, :]).astype(jnp.int32), axis=1) - 1
        placed = wanted[:, None] & (position[:, None] == flat_places[None, :])
        packed_ids = jnp.sum(jnp.where(placed, held_slots[:, None], 0), axis=0)
        packed_owner = jnp.sum(jnp.where(placed, flat_owner[:, None], 0), axis=0)
        live_tiles = jnp.sum(wanted.astype(jnp.int32))

        def one_tile(tile_index, loop_state):
            query_grad, key_grads = loop_state
            key_block = packed_ids[tile_index]
            owner_block = packed_owner[tile_index]
            key_start = (
                key_block // (block_count * ka_count) * block_count + key_block % block_count
            ) * block_rows
            pair_tile = lax.dynamic_slice_in_dim(column_keys, key_start, block_rows, 0)
            key_tile = pair_tile[:, :head_width]
            value_tile = pair_tile[:, head_width:]
            query_tile = held_query.reshape(block_rows, part_heads, head_width)
            grad_tile = held_grad.reshape(block_rows, part_heads, head_width)
            scores = (
                jnp.einsum("rhd,cd->hrc", query_tile, key_tile, preferred_element_type=jnp.float32)
                * score_scale
            )
            query_pos = (first_block + owner_block) * block_rows + row_offsets
            key_pos = key_block * block_rows + row_offsets
            allowed = key_pos[None, :] <= query_pos[:, None]
            probs_full = jnp.exp(
                jnp.where(allowed[None], scores - total_rows[:, :, None], VERY_LOW)
            )
            prob_grads = jnp.einsum(
                "rhd,cd->hrc", grad_tile, value_tile, preferred_element_type=jnp.float32
            )
            score_grads = probs_full * (prob_grads - delta_rows[:, :, None])
            rounded_probs = probs_full.astype(jnp.bfloat16)
            rounded_grads = score_grads.astype(jnp.bfloat16)
            value_part = jnp.einsum(
                "hrc,rhd->cd", rounded_probs, grad_tile, preferred_element_type=jnp.float32
            )
            key_part = (
                jnp.einsum(
                    "hrc,rhd->cd", rounded_grads, query_tile, preferred_element_type=jnp.float32
                )
                * score_scale
            )
            query_part = (
                jnp.einsum(
                    "hrc,cd->rhd", rounded_grads, key_tile, preferred_element_type=jnp.float32
                )
                * score_scale
            )
            old_query = query_grad
            query_grad = old_query + query_part.reshape(block_rows, -1)
            old_keys = lax.dynamic_slice_in_dim(key_grads, key_start, block_rows, 0)
            key_grads = lax.dynamic_update_slice_in_dim(
                key_grads, old_keys + jnp.concatenate([key_part, value_part], 1), key_start, 0
            )
            return (query_grad, key_grads)

        return lax.fori_loop(0, live_tiles, one_tile, (query_grad, key_grads))

    query_part = query_rows
    grad_zero = jnp.zeros(query_part.shape, jnp.float32)
    row_stack = jnp.stack([query_part, out_grads, outputs])
    query_grad = grad_zero
    stat_stack = log_totals[None]

    def forward_hop(hop_index, loop_state):
        row_stack, query_grad, stat_stack, key_grads = loop_state
        anchor = (ka_index - hop_index) % ka_count
        query_grad, key_grads = visit_block(row_stack, query_grad, stat_stack, anchor, key_grads)
        row_stack = passed_along(row_stack, "ka", 1)
        query_grad, stat_stack = passed_along((query_grad, stat_stack), "ka", 1)
        return (row_stack, query_grad, stat_stack, key_grads)

    row_stack, query_grad, stat_stack, key_grads = lax.fori_loop(
        0, ka_count - 1, forward_hop, (row_stack, query_grad, stat_stack, key_grads)
    )
    query_grad, key_grads = visit_block(
        row_stack, query_grad, stat_stack, (ka_index + 1) % ka_count, key_grads
    )
    query_grad = passed_along(query_grad, "ka", 1)
    owned_grads = lax.psum_scatter(key_grads, "pb", scatter_dimension=0, tiled=True)
    return (query_grad, owned_grads[:, :head_width], owned_grads[:, head_width:])


MESH = pl.DeviceIdType.MESH
VMEM_BUDGET = 40 << 20


NT = (((1,), (1,)), ((), ()))
TN = (((0,), (0,)), ((), ()))
INFO = 128
INFO_C, INFO_P, KEY_P, KEY_C, VALUE_C, VALUE_P, KGRAD_P, KGRAD_C, VGRAD_C, VGRAD_P = range(10)


def tile_scores(key_tile, query_flip, total_row, scale):
    scores = jnp.dot(key_tile, query_flip, preferred_element_type=jnp.float32) * scale
    return scores - total_row


def tile_score_grads(probs, value_tile, grad_stack, delta_row):
    prob_grads = lax.dot_general(value_tile, grad_stack, NT, preferred_element_type=jnp.float32)
    return (probs * (prob_grads - delta_row)).astype(jnp.bfloat16)


def query_share(score_grads, key_tile, scale):
    return lax.dot_general(score_grads, key_tile, TN, preferred_element_type=jnp.float32) * scale


def whole_kernel(
    ka_count, inner, line_count,
    query_hbm, key_hbm, value_hbm, out_hbm, grad_hbm, total_hbm, selected_hbm, counts_hbm,
    query_grad_ref, key_grad_ref, value_grad_ref,
    query_ref, out_ref, grad_ref, total_ref, selected_ref, counts_ref,
    key_own, value_own, key_plane, value_column,
    key_picked, value_picked, key_in, value_in,
    key_part, value_part, kgrad_plane, vgrad_column,
    kgrad_sum, vgrad_sum, kgrad_matrix, vgrad_matrix, kgrad_in, vgrad_in,
    own_info, plane_info, column_info, query_stack, grad_stack, query_flip, grad_flip, query_acc, key_acc, value_acc,
    send_sem, recv_sem, load_sem,
):
    bf, f32 = jnp.bfloat16, jnp.float32
    plane_count = inner * ka_count
    column_count = 2 * line_count
    pb_index, ka_index = lax.axis_index("pb"), lax.axis_index("ka")
    line = lax.div(pb_index, inner)
    row = lax.rem(pb_index, inner)
    place = row * ka_count + ka_index
    chip, core = lax.div(place, 2), lax.rem(place, 2)
    member = line * 2 + core
    block_rows, head_width = key_hbm.shape
    half_rows = block_rows // 2
    heads = total_hbm.shape[0]
    scale = head_width ** (-0.5)
    block = line * plane_count + place

    def half(which):
        if isinstance(which, int):
            return pl.ds(which * half_rows, half_rows)
        return pl.ds(pl.multiple_of(which * half_rows, half_rows), half_rows)

    def others(me, count):
        return [other + lax.convert_element_type(other >= me, jnp.int32) for other in range(count - 1)]

    def plane_of(places):
        return [
            (peer, (line * inner + lax.div(peer, ka_count), lax.rem(peer, ka_count)))
            for peer in [place, *places]
        ]

    def column_of(lines):
        peers = [member, line * 2 + 1 - core]
        for other in lines:
            peers += [other * 2 + 1 - core, other * 2 + core]
        return [
            (peer, (
                lax.div(peer, 2) * inner + lax.div(chip * 2 + lax.rem(peer, 2), ka_count),
                lax.rem(chip * 2 + lax.rem(peer, 2), ka_count),
            ))
            for peer in peers
        ]

    rising = others(line, line_count)
    places = others(place, plane_count)
    plane = plane_of(places)
    plane_back = plane_of(places[::-1])
    column = column_of(rising)
    column_back = column_of(rising[::-1])

    barrier = pltpu.get_barrier_semaphore()
    for group in (column, plane):
        for _, device in group[:0:-1]:
            pl.semaphore_signal(barrier, inc=1, device_id=device, device_id_type=MESH)
    loads = [
        pltpu.make_async_copy(source, target, load_sem.at[index])
        for index, (source, target) in enumerate((
            (selected_hbm, selected_ref), (counts_hbm, counts_ref),
            (key_hbm, key_own), (value_hbm, value_own),
            (query_hbm, query_ref), (grad_hbm, grad_ref), (out_hbm, out_ref), (total_hbm, total_ref),
        ))
    ]
    for load in loads:
        load.start()

    loads[0].wait()
    loads[1].wait()
    target = jnp.where(counts_ref[0] > 1, selected_ref[0, 1], -1)
    own_line = jnp.full(own_info.shape, target, jnp.int32)
    own_info[...] = own_line
    plane_info[place] = own_line
    column_info[member] = own_line

    sent = []

    def send(leg, device, source, target):
        pltpu.make_async_remote_copy(
            src_ref=source, dst_ref=target, send_sem=send_sem.at[leg], recv_sem=recv_sem.at[leg],
            device_id=device, device_id_type=MESH,
        ).start()

    def whole_leg(leg, group, held):
        units = held.at[pl.ds(0, len(group) - 1)]
        return pltpu.make_async_remote_copy(
            src_ref=units, dst_ref=units, send_sem=send_sem.at[leg], recv_sem=recv_sem.at[leg],
            device_id=group[1][1], device_id_type=MESH,
        )

    def arrive(leg, group, held):
        whole_leg(leg, group, held).wait_recv()

    def settle():
        for started in sent:
            whole_leg(*started).wait_send()
        sent.clear()

    def farthest_first(group):
        return [(offset, *group[offset]) for offset in range(len(group) - 1, 0, -1)]

    for load in loads[2:4]:
        load.wait()
    key_plane[place] = key_own[half(core), :]
    value_column[member] = value_own[half(core), :]
    pl.semaphore_wait(barrier, plane_count + column_count - 2)
    for _, _, device in farthest_first(column_back):
        send(INFO_C, device, own_info, column_info.at[member])
    for _, peer, device in farthest_first(plane):
        send(KEY_P, device, key_own.at[half(lax.rem(peer, 2))], key_plane.at[place])
    for _, peer, device in farthest_first(column):
        send(VALUE_C, device, value_own.at[half(lax.rem(peer, 2))], value_column.at[member])
    for _, _, device in farthest_first(plane):
        send(INFO_P, device, own_info, plane_info.at[place])
    sent += [(INFO_C, column, column_info), (VALUE_C, column, value_column)]
    sent += [(KEY_P, plane, key_plane), (INFO_P, plane, plane_info)]

    for load in loads[4:]:
        load.wait()
    deltas = []
    for head in range(heads):
        columns = pl.ds(head * head_width, head_width)
        rows = pl.ds(head * block_rows, block_rows)
        query_stack[rows, :] = query_ref[:, columns]
        grad_stack[rows, :] = grad_ref[:, columns]
        query_flip[:, rows] = query_ref[:, columns].T
        grad_flip[:, rows] = grad_ref[:, columns].T
        product = grad_ref[:, columns].astype(f32) * out_ref[:, columns].astype(f32)
        deltas.append(jnp.sum(product.T, axis=0, keepdims=True))
    delta_row = jnp.concatenate(deltas, axis=1)
    total_row = jnp.concatenate([total_ref[head : head + 1, :] for head in range(heads)], axis=1)
    stack_shape = (block_rows, heads * block_rows)
    key_offset = lax.broadcasted_iota(jnp.int32, stack_shape, 0)
    query_offset = lax.rem(lax.broadcasted_iota(jnp.int32, stack_shape, 1), block_rows)

    arrive(INFO_C, column, column_info)
    column_targets = [column_info[peer][0, 0] for peer, _ in column]
    arrive(KEY_P, plane, key_plane)
    for offset, _, device in farthest_first(column):
        key_picked[offset] = key_plane[lax.rem(jnp.maximum(column_targets[offset], 0), plane_count)]
        send(KEY_C, device, key_picked.at[offset], key_in.at[member])
    listed = jnp.maximum(target, 0)
    key_in[member] = key_plane[lax.rem(listed, plane_count)]

    arrive(INFO_P, plane, plane_info)
    plane_targets = [plane_info[peer][0, 0] for peer, _ in plane]
    arrive(VALUE_C, column, value_column)
    for offset, _, device in farthest_first(plane):
        wanted = jnp.maximum(plane_targets[offset], 0)
        value_picked[offset] = value_column[lax.div(wanted, plane_count) * 2 + lax.rem(wanted, 2)]
        send(VALUE_P, device, value_picked.at[offset], value_in.at[place])
    value_in[place] = value_column[lax.div(listed, plane_count) * 2 + lax.rem(listed, 2)]
    settle()
    sent += [(KEY_C, column, key_picked), (VALUE_P, plane, value_picked)]

    listed_total = jnp.where(target >= 0, total_row, -VERY_LOW)

    plane_sources = [plane_info[source][0, 0] for source in range(plane_count)]
    column_sources = [column_info[source][0, 0] for source in range(column_count)]
    own_key = key_own[...]
    scores = tile_scores(own_key, query_flip[...], total_row, scale)
    probs = jnp.exp(jnp.where(key_offset <= query_offset, scores, VERY_LOW))
    value_acc[...] = jnp.dot(probs.astype(bf), grad_stack[...], preferred_element_type=f32)
    score_grads = tile_score_grads(probs, value_own[...], grad_stack[...], delta_row)
    query_acc[...] = query_share(score_grads, own_key, scale)
    key_acc[...] = jnp.dot(score_grads, query_stack[...], preferred_element_type=f32) * scale

    def listed_tile(halves, pair):
        return jnp.concatenate([halves[2 * pair], halves[2 * pair + 1]], axis=0)

    arrive(VALUE_P, plane, value_in)
    value_tile = listed_tile(value_in, lax.div(lax.rem(listed, plane_count), 2))
    prob_grads = jnp.dot(value_tile, grad_flip[...], preferred_element_type=f32) - delta_row
    arrive(KEY_C, column, key_in)
    key_tile = listed_tile(key_in, lax.div(listed, plane_count))
    probs = jnp.exp(tile_scores(key_tile, query_flip[...], listed_total, scale))
    value_part[...] = jnp.dot(probs.astype(bf), grad_stack[...], preferred_element_type=f32).astype(bf)
    score_grads = (probs * prob_grads).astype(bf)
    key_part[...] = (jnp.dot(score_grads, query_stack[...], preferred_element_type=f32) * scale).astype(bf)
    for _, peer, device in farthest_first(column_back):
        send(VGRAD_C, device, value_part.at[half(lax.rem(peer, 2))], vgrad_column.at[member])
    for _, peer, device in farthest_first(plane_back):
        send(KGRAD_P, device, key_part.at[half(lax.rem(peer, 2))], kgrad_plane.at[place])
    vgrad_column[member] = value_part[half(core), :]
    kgrad_plane[place] = key_part[half(core), :]
    settle()
    sent += [(VGRAD_C, column, vgrad_column), (KGRAD_P, plane, kgrad_plane)]
    query_acc[...] += query_share(score_grads, key_tile, scale)
    for head in range(heads):
        query_grad_ref[:, pl.ds(head * head_width, head_width)] = query_acc[
            pl.ds(head * block_rows, block_rows), :
        ]

    def owner_sum(owner, targets, held):
        terms = [jnp.where(aimed == owner, held[source].astype(f32), 0.0) for source, aimed in enumerate(targets)]
        for term in terms[1:]:
            terms[0] = terms[0] + term
        return terms[0].astype(bf)

    arrive(KGRAD_P, plane, kgrad_plane)
    for offset, peer, device in farthest_first(column_back):
        owner = lax.div(peer, 2) * plane_count + chip * 2 + lax.rem(peer, 2)
        kgrad_sum[offset] = owner_sum(owner, plane_sources, kgrad_plane)
        send(KGRAD_C, device, kgrad_sum.at[offset], kgrad_in.at[member])
    kgrad_in[member] = owner_sum(block, plane_sources, kgrad_plane)

    arrive(VGRAD_C, column, vgrad_column)
    for offset, peer, device in farthest_first(plane_back):
        vgrad_sum[offset] = owner_sum(line * plane_count + peer, column_sources, vgrad_column)
        send(VGRAD_P, device, vgrad_sum.at[offset], vgrad_in.at[place])
    vgrad_in[place] = owner_sum(block, column_sources, vgrad_column)
    sent += [(KGRAD_C, column, kgrad_sum), (VGRAD_P, plane, vgrad_sum)]
    settle()

    def grown(total, halves):
        parts = halves[...].astype(f32).reshape(halves.shape[0] // 2, block_rows, head_width)
        return total + jnp.sum(parts, axis=0)

    arrive(KGRAD_C, column, kgrad_in)
    key_grad_ref[...] = grown(key_acc[...], kgrad_in)
    arrive(VGRAD_P, plane, vgrad_in)
    value_grad_ref[...] = grown(value_acc[...], vgrad_in)


def kernel_shards(query_rows, key_rows, value_rows, outputs, out_grads, log_totals, selected, counts):
    ka_count, pb_count = lax.axis_size("ka"), lax.axis_size("pb")
    inner = 2 if pb_count % 2 == 0 else 1
    line_count, plane_count = pb_count // inner, inner * ka_count
    column_count = 2 * line_count
    block_rows, head_width = key_rows.shape
    heads = log_totals.shape[0]
    tile = key_rows.shape
    half_rows = block_rows // 2
    part = (half_rows, head_width)
    dma = pltpu.SemaphoreType.DMA
    vmem = pl.BlockSpec(memory_space=pltpu.VMEM)
    hbm = pl.BlockSpec(memory_space=pl.ANY)
    bf, f32 = jnp.bfloat16, jnp.float32
    shapes = (query_rows.shape, key_rows.shape, value_rows.shape)
    held = pl.pallas_call(
        functools.partial(whole_kernel, ka_count, inner, line_count),
        out_shape=tuple(pltpu.VMEM(shape, f32) for shape in shapes),
        in_specs=[hbm] * 8,
        out_specs=(vmem, vmem, vmem),
        scratch_shapes=[
            pltpu.VMEM(query_rows.shape, bf),
            pltpu.VMEM(query_rows.shape, bf),
            pltpu.VMEM(query_rows.shape, bf),
            pltpu.VMEM(log_totals.shape, f32),
            pltpu.SMEM(selected.shape, jnp.int32),
            pltpu.SMEM(counts.shape, jnp.int32),
            pltpu.VMEM(tile, bf),
            pltpu.VMEM(tile, bf),
            pltpu.VMEM((plane_count, *part), bf),
            pltpu.VMEM((column_count, *part), bf),
            pltpu.VMEM((column_count, *part), bf),
            pltpu.VMEM((plane_count, *part), bf),
            pltpu.VMEM((column_count, *part), bf),
            pltpu.VMEM((plane_count, *part), bf),
            pltpu.VMEM(tile, bf),
            pltpu.VMEM(tile, bf),
            pltpu.VMEM((plane_count, *part), bf),
            pltpu.VMEM((column_count, *part), bf),
            pltpu.VMEM((column_count, *part), bf),
            pltpu.VMEM((plane_count, *part), bf),
            pltpu.VMEM((column_count * half_rows, plane_count * half_rows), bf),
            pltpu.VMEM((plane_count * half_rows, column_count * half_rows), bf),
            pltpu.VMEM((column_count, *part), bf),
            pltpu.VMEM((plane_count, *part), bf),
            pltpu.VMEM((1, INFO), jnp.int32),
            pltpu.VMEM((plane_count, 1, INFO), jnp.int32),
            pltpu.VMEM((column_count, 1, INFO), jnp.int32),
            pltpu.VMEM((heads * block_rows, head_width), bf),
            pltpu.VMEM((heads * block_rows, head_width), bf),
            pltpu.VMEM((head_width, heads * block_rows), bf),
            pltpu.VMEM((head_width, heads * block_rows), bf),
            pltpu.VMEM((heads * block_rows, head_width), f32),
            pltpu.VMEM(tile, f32),
            pltpu.VMEM(tile, f32),
            dma((10,)),
            dma((10,)),
            dma((8,)),
        ],
        compiler_params=pltpu.CompilerParams(collective_id=0, has_side_effects=True),
    )(query_rows, key_rows, value_rows, outputs, out_grads, log_totals, selected, counts)
    return pl.pallas_call(
        write_kernel,
        out_shape=tuple(jax.ShapeDtypeStruct(shape, f32) for shape in shapes),
        in_specs=[vmem] * 3,
        out_specs=(hbm, hbm, hbm),
        scratch_shapes=[dma((3,))],
    )(*[pltpu.with_memory_space_constraint(part, pltpu.VMEM) for part in held])


def write_kernel(*refs):
    sources, targets, sem = refs[:3], refs[3:6], refs[6]
    stores = [pltpu.make_async_copy(*pair, sem.at[i]) for i, pair in enumerate(zip(sources, targets))]
    for store in stores:
        store.start()
    for store in stores:
        store.wait()


def fits_kernel(query_rows, key_rows, value_rows, outputs, out_grads, log_totals, selected, counts):
    pb_count, ka_count = lax.axis_size("pb"), lax.axis_size("ka")
    block_rows, head_width = key_rows.shape
    inner = 2 if pb_count % 2 == 0 else 1
    tile_bytes = 2 * block_rows * head_width
    tiles = 6 * (pb_count // inner + inner * ka_count)
    return (
        selected.shape[0] == 1
        and selected.shape[1] == 2
        and ka_count % 2 == 0
        and pb_count > inner
        and block_rows == head_width == 128
        and tiles * tile_bytes < VMEM_BUDGET
    )


def either(*arrays):
    return kernel_shards(*arrays) if fits_kernel(*arrays) else shards(*arrays)


def solution(mesh):
    return jax.shard_map(
        either,
        mesh=mesh,
        in_specs=(
            P(("pb", "ka"), None),
            P(("pb", "ka"), None),
            P(("pb", "ka"), None),
            P(("pb", "ka"), None),
            P(("pb", "ka"), None),
            P(None, ("pb", "ka")),
            P(("pb", "ka"), None),
            P(("pb", "ka")),
        ),
        out_specs=(P(("pb", "ka"), None), P(("pb", "ka"), None), P(("pb", "ka"), None)),
        check_vma=False,
    )
```

```python
import functools

import jax
import jax.numpy as jnp
from jax import lax
from jax.experimental import pallas as pl
from jax.experimental.pallas import tpu as pltpu
from jax.sharding import PartitionSpec as P

VERY_LOW = -1e30


def passed_along(value, axis, steps):
    count = lax.axis_size(axis)
    pairs = [(source, (source + steps) % count) for source in range(count)]
    return lax.ppermute(value, axis, pairs)


def head_sums(grad_rows, out_rows, head_width):
    row_total = grad_rows.shape[0]
    part_heads = grad_rows.shape[1] // head_width
    product = grad_rows.astype(jnp.float32) * out_rows.astype(jnp.float32)
    return jnp.sum(product.reshape(row_total, part_heads, head_width), axis=2).T


def shards(query_rows, key_rows, value_rows, outputs, out_grads, log_totals, selected, counts):
    ka_count = lax.axis_size("ka")
    ka_index = lax.axis_index("ka")
    pb_index = lax.axis_index("pb")
    block_count = selected.shape[0]
    slot_count = selected.shape[1]
    head_width = key_rows.shape[1]
    block_rows = query_rows.shape[0] // block_count
    score_scale = head_width ** (-0.5)
    key_pairs = jnp.concatenate([key_rows, value_rows], 1)
    column_keys = lax.all_gather(key_pairs, "pb", axis=0, tiled=True)
    peer_slots, peer_counts = (
        lax.all_gather(selected, "ka", axis=0, tiled=True),
        lax.all_gather(counts, "ka", axis=0, tiled=True),
    )
    key_grads = jnp.zeros((column_keys.shape[0], 2 * head_width), jnp.float32)
    row_offsets = jnp.arange(block_rows, dtype=jnp.int32)
    flat_owner = jnp.repeat(jnp.arange(block_count, dtype=jnp.int32), slot_count)
    flat_slot = jnp.tile(jnp.arange(slot_count, dtype=jnp.int32), block_count)
    flat_places = jnp.arange(block_count * slot_count, dtype=jnp.int32)

    def visit_block(row_stack, query_grad, stat_stack, anchor, key_grads):
        held_query = row_stack[0]
        held_grad = row_stack[1]
        total_rows = stat_stack[0]
        delta_rows = head_sums(row_stack[1], row_stack[2], head_width)
        part_heads = total_rows.shape[0]
        held_slots = lax.dynamic_slice_in_dim(
            peer_slots, anchor * block_count, block_count, 0
        ).reshape(-1)
        held_counts = jnp.repeat(
            lax.dynamic_slice_in_dim(peer_counts, anchor * block_count, block_count, 0), slot_count
        )
        first_block = (pb_index * ka_count + anchor) * block_count
        wanted = (flat_slot < held_counts) & (held_slots // block_count % ka_count == ka_index)
        earlier = flat_places[None, :] <= flat_places[:, None]
        position = jnp.sum((earlier & wanted[None, :]).astype(jnp.int32), axis=1) - 1
        placed = wanted[:, None] & (position[:, None] == flat_places[None, :])
        packed_ids = jnp.sum(jnp.where(placed, held_slots[:, None], 0), axis=0)
        packed_owner = jnp.sum(jnp.where(placed, flat_owner[:, None], 0), axis=0)
        live_tiles = jnp.sum(wanted.astype(jnp.int32))

        def one_tile(tile_index, loop_state):
            query_grad, key_grads = loop_state
            key_block = packed_ids[tile_index]
            owner_block = packed_owner[tile_index]
            key_start = (
                key_block // (block_count * ka_count) * block_count + key_block % block_count
            ) * block_rows
            pair_tile = lax.dynamic_slice_in_dim(column_keys, key_start, block_rows, 0)
            key_tile = pair_tile[:, :head_width]
            value_tile = pair_tile[:, head_width:]
            query_tile = held_query.reshape(block_rows, part_heads, head_width)
            grad_tile = held_grad.reshape(block_rows, part_heads, head_width)
            scores = (
                jnp.einsum("rhd,cd->hrc", query_tile, key_tile, preferred_element_type=jnp.float32)
                * score_scale
            )
            query_pos = (first_block + owner_block) * block_rows + row_offsets
            key_pos = key_block * block_rows + row_offsets
            allowed = key_pos[None, :] <= query_pos[:, None]
            probs_full = jnp.exp(
                jnp.where(allowed[None], scores - total_rows[:, :, None], VERY_LOW)
            )
            prob_grads = jnp.einsum(
                "rhd,cd->hrc", grad_tile, value_tile, preferred_element_type=jnp.float32
            )
            score_grads = probs_full * (prob_grads - delta_rows[:, :, None])
            rounded_probs = probs_full.astype(jnp.bfloat16)
            rounded_grads = score_grads.astype(jnp.bfloat16)
            value_part = jnp.einsum(
                "hrc,rhd->cd", rounded_probs, grad_tile, preferred_element_type=jnp.float32
            )
            key_part = (
                jnp.einsum(
                    "hrc,rhd->cd", rounded_grads, query_tile, preferred_element_type=jnp.float32
                )
                * score_scale
            )
            query_part = (
                jnp.einsum(
                    "hrc,cd->rhd", rounded_grads, key_tile, preferred_element_type=jnp.float32
                )
                * score_scale
            )
            old_query = query_grad
            query_grad = old_query + query_part.reshape(block_rows, -1)
            old_keys = lax.dynamic_slice_in_dim(key_grads, key_start, block_rows, 0)
            key_grads = lax.dynamic_update_slice_in_dim(
                key_grads, old_keys + jnp.concatenate([key_part, value_part], 1), key_start, 0
            )
            return (query_grad, key_grads)

        return lax.fori_loop(0, live_tiles, one_tile, (query_grad, key_grads))

    query_part = query_rows
    grad_zero = jnp.zeros(query_part.shape, jnp.float32)
    row_stack = jnp.stack([query_part, out_grads, outputs])
    query_grad = grad_zero
    stat_stack = log_totals[None]

    def forward_hop(hop_index, loop_state):
        row_stack, query_grad, stat_stack, key_grads = loop_state
        anchor = (ka_index - hop_index) % ka_count
        query_grad, key_grads = visit_block(row_stack, query_grad, stat_stack, anchor, key_grads)
        row_stack = passed_along(row_stack, "ka", 1)
        query_grad, stat_stack = passed_along((query_grad, stat_stack), "ka", 1)
        return (row_stack, query_grad, stat_stack, key_grads)

    row_stack, query_grad, stat_stack, key_grads = lax.fori_loop(
        0, ka_count - 1, forward_hop, (row_stack, query_grad, stat_stack, key_grads)
    )
    query_grad, key_grads = visit_block(
        row_stack, query_grad, stat_stack, (ka_index + 1) % ka_count, key_grads
    )
    query_grad = passed_along(query_grad, "ka", 1)
    owned_grads = lax.psum_scatter(key_grads, "pb", scatter_dimension=0, tiled=True)
    return (query_grad, owned_grads[:, :head_width], owned_grads[:, head_width:])


MESH = pl.DeviceIdType.MESH
VMEM_BUDGET = 40 << 20


NT = (((1,), (1,)), ((), ()))
TN = (((0,), (0,)), ((), ()))
INFO = 128
INFO_C, INFO_P, KEY_P, KEY_C, VALUE_C, VALUE_P, KGRAD_P, KGRAD_C, VGRAD_C, VGRAD_P = range(10)


def tile_scores(key_tile, query_flip, total_row, scale):
    scores = jnp.dot(key_tile, query_flip, preferred_element_type=jnp.float32) * scale
    return scores - total_row


def tile_score_grads(probs, value_tile, grad_stack, delta_row):
    prob_grads = lax.dot_general(value_tile, grad_stack, NT, preferred_element_type=jnp.float32)
    return (probs * (prob_grads - delta_row)).astype(jnp.bfloat16)


def query_share(score_grads, key_tile, scale):
    return lax.dot_general(score_grads, key_tile, TN, preferred_element_type=jnp.float32) * scale


def whole_kernel(
    ka_count, inner, line_count,
    query_hbm, key_hbm, value_hbm, out_hbm, grad_hbm, total_hbm, selected_hbm, counts_hbm,
    query_grad_ref, key_grad_ref, value_grad_ref,
    query_ref, out_ref, grad_ref, total_ref, selected_ref,
    key_own, value_own, key_plane, value_column,
    key_picked, value_picked, key_in, value_in,
    key_part, value_part, kgrad_plane, vgrad_column,
    kgrad_sum, vgrad_sum, kgrad_matrix, vgrad_matrix, kgrad_in, vgrad_in,
    own_info, plane_info, column_info, query_stack, grad_stack, query_flip, grad_flip, query_acc, key_acc, value_acc,
    send_sem, recv_sem, load_sem,
):
    bf, f32 = jnp.bfloat16, jnp.float32
    plane_count = inner * ka_count
    column_count = 2 * line_count
    pb_index, ka_index = lax.axis_index("pb"), lax.axis_index("ka")
    line = lax.div(pb_index, inner)
    row = lax.rem(pb_index, inner)
    place = row * ka_count + ka_index
    chip, core = lax.div(place, 2), lax.rem(place, 2)
    member = line * 2 + core
    block_rows, head_width = key_hbm.shape
    half_rows = block_rows // 2
    heads = total_hbm.shape[0]
    scale = head_width ** (-0.5)
    block = line * plane_count + place

    def half(which):
        if isinstance(which, int):
            return pl.ds(which * half_rows, half_rows)
        return pl.ds(pl.multiple_of(which * half_rows, half_rows), half_rows)

    def others(me, count):
        return [other + lax.convert_element_type(other >= me, jnp.int32) for other in range(count - 1)]

    def plane_of(places):
        return [
            (peer, (line * inner + lax.div(peer, ka_count), lax.rem(peer, ka_count)))
            for peer in [place, *places]
        ]

    def column_device(other, side):
        there = chip * 2 + side
        return other * inner + lax.div(there, ka_count), lax.rem(there, ka_count)

    def to_core_peer(act):
        act(line, 1 - core, column_device(line, 1 - core))

    def to_above(act):
        for other in range(line_count - 1, 0, -1):
            @pl.when(other > line)
            def _():
                for side in range(2):
                    act(other, side, column_device(other, side))
        to_core_peer(act)

    def to_below(act):
        for other in range(line_count - 1):
            @pl.when(other < line)
            def _():
                for side in range(2):
                    act(other, side, column_device(other, side))
        to_core_peer(act)

    places = others(place, plane_count)
    plane = plane_of(places)
    plane_back = plane_of(places[::-1])

    barrier = pltpu.get_barrier_semaphore()
    for other in range(line_count):
        @pl.when(other != line)
        def _():
            for side in range(2):
                pl.semaphore_signal(barrier, inc=1, device_id=column_device(other, side), device_id_type=MESH)
    for _, device in plane[:0:-1]:
        pl.semaphore_signal(barrier, inc=1, device_id=device, device_id_type=MESH)
    loads = [
        pltpu.make_async_copy(source, target, load_sem.at[index])
        for index, (source, target) in enumerate((
            (selected_hbm, selected_ref),
            (key_hbm, key_own), (value_hbm, value_own),
            (query_hbm, query_ref), (grad_hbm, grad_ref), (out_hbm, out_ref), (total_hbm, total_ref),
        ))
    ]
    for load in loads:
        load.start()

    loads[0].wait()
    target = jnp.where(counts_hbm[0] > 1, selected_ref[0, 1], -1)
    own_line = jnp.full(own_info.shape, target, jnp.int32)
    own_info[...] = own_line
    plane_info[place] = own_line
    column_info[member] = own_line

    sent = []

    def send(leg, device, source, target):
        pltpu.make_async_remote_copy(
            src_ref=source, dst_ref=target, send_sem=send_sem.at[leg], recv_sem=recv_sem.at[leg],
            device_id=device, device_id_type=MESH,
        ).start()

    ABOVE, BELOW, PLANE = range(3)

    def whole_leg(leg, reach, held, act):
        def wait(count):
            units = held.at[pl.ds(0, count)]
            act(pltpu.make_async_remote_copy(
                src_ref=units, dst_ref=units, send_sem=send_sem.at[leg], recv_sem=recv_sem.at[leg],
                device_id=plane[1][1], device_id_type=MESH,
            ))

        if reach == PLANE:
            wait(plane_count - 1)
        else:
            for here in range(line_count):
                lines = here if reach == BELOW else line_count - 1 - here
                pl.when(line == here)(functools.partial(wait, 2 * lines + 1))

    def arrive(leg, reach, held):
        whole_leg(leg, reach, held, lambda copy: copy.wait_recv())

    def settle():
        for started in sent:
            whole_leg(*started, lambda copy: copy.wait_send())
        sent.clear()

    def farthest_first(group):
        return [(offset, *group[offset]) for offset in range(len(group) - 1, 0, -1)]

    for load in loads[1:3]:
        load.wait()
    key_plane[place] = key_own[half(core), :]
    value_column[member] = value_own[half(core), :]
    for load in loads[3:]:
        load.wait()
    deltas = []
    for head in range(heads):
        columns = pl.ds(head * head_width, head_width)
        rows = pl.ds(head * block_rows, block_rows)
        query_stack[rows, :] = query_ref[:, columns]
        grad_stack[rows, :] = grad_ref[:, columns]
        query_flip[:, rows] = query_ref[:, columns].T
        grad_flip[:, rows] = grad_ref[:, columns].T
        product = grad_ref[:, columns].astype(f32) * out_ref[:, columns].astype(f32)
        deltas.append(jnp.sum(product.T, axis=0, keepdims=True))
    delta_row = jnp.concatenate(deltas, axis=1)
    total_row = jnp.concatenate([total_ref[head : head + 1, :] for head in range(heads)], axis=1)
    stack_shape = (block_rows, heads * block_rows)
    key_offset = lax.broadcasted_iota(jnp.int32, stack_shape, 0)
    query_offset = lax.rem(lax.broadcasted_iota(jnp.int32, stack_shape, 1), block_rows)
    nothing = jnp.zeros((half_rows, head_width), bf)
    for other in range(line_count):
        @pl.when(other > line)
        def _():
            for side in range(2):
                value_column[other * 2 + side] = nothing
                key_in[other * 2 + side] = nothing

        @pl.when(other < line)
        def _():
            for side in range(2):
                column_info[other * 2 + side] = jnp.full(own_info.shape, -1, jnp.int32)
                vgrad_column[other * 2 + side] = nothing
                kgrad_in[other * 2 + side] = nothing

    pl.semaphore_wait(barrier, plane_count + column_count - 3)
    to_above(lambda other, side, device: send(VALUE_C, device, value_own.at[half(side)], value_column.at[member]))
    for _, peer, device in farthest_first(plane):
        send(KEY_P, device, key_own.at[half(lax.rem(peer, 2))], key_plane.at[place])
    to_below(lambda other, side, device: send(INFO_C, device, own_info, column_info.at[member]))
    for _, _, device in farthest_first(plane):
        send(INFO_P, device, own_info, plane_info.at[place])
    sent += [(INFO_C, BELOW, column_info), (VALUE_C, ABOVE, value_column)]
    sent += [(KEY_P, PLANE, key_plane), (INFO_P, PLANE, plane_info)]

    arrive(INFO_C, ABOVE, column_info)
    arrive(KEY_P, PLANE, key_plane)

    def pick_key(other, side, device):
        slot = other * 2 + side
        key_picked[slot] = key_plane[lax.rem(jnp.maximum(column_info[slot][0, 0], 0), plane_count)]
        send(KEY_C, device, key_picked.at[slot], key_in.at[member])

    to_above(pick_key)
    listed = jnp.maximum(target, 0)
    key_in[member] = key_plane[lax.rem(listed, plane_count)]

    arrive(INFO_P, PLANE, plane_info)
    plane_targets = [plane_info[peer][0, 0] for peer, _ in plane]
    arrive(VALUE_C, BELOW, value_column)
    for offset, _, device in farthest_first(plane):
        wanted = jnp.maximum(plane_targets[offset], 0)
        value_picked[offset] = value_column[lax.div(wanted, plane_count) * 2 + lax.rem(wanted, 2)]
        send(VALUE_P, device, value_picked.at[offset], value_in.at[place])
    value_in[place] = value_column[lax.div(listed, plane_count) * 2 + lax.rem(listed, 2)]
    settle()
    sent += [(KEY_C, ABOVE, key_picked), (VALUE_P, PLANE, value_picked)]

    listed_total = jnp.where(target >= 0, total_row, -VERY_LOW)

    plane_sources = [plane_info[source][0, 0] for source in range(plane_count)]
    column_sources = [column_info[source][0, 0] for source in range(column_count)]
    own_key = key_own[...]
    scores = tile_scores(own_key, query_flip[...], total_row, scale)
    probs = jnp.exp(jnp.where(key_offset <= query_offset, scores, VERY_LOW))
    value_acc[...] = jnp.dot(probs.astype(bf), grad_stack[...], preferred_element_type=f32)
    score_grads = tile_score_grads(probs, value_own[...], grad_stack[...], delta_row)
    query_acc[...] = query_share(score_grads, own_key, scale)
    key_acc[...] = jnp.dot(score_grads, query_stack[...], preferred_element_type=f32) * scale

    def listed_tile(halves, pair):
        return jnp.concatenate([halves[2 * pair], halves[2 * pair + 1]], axis=0)

    arrive(VALUE_P, PLANE, value_in)
    value_tile = listed_tile(value_in, lax.div(lax.rem(listed, plane_count), 2))
    prob_grads = jnp.dot(value_tile, grad_flip[...], preferred_element_type=f32) - delta_row
    arrive(KEY_C, BELOW, key_in)
    key_tile = listed_tile(key_in, lax.div(listed, plane_count))
    probs = jnp.exp(tile_scores(key_tile, query_flip[...], listed_total, scale))
    value_part[...] = jnp.dot(probs.astype(bf), grad_stack[...], preferred_element_type=f32).astype(bf)
    score_grads = (probs * prob_grads).astype(bf)
    key_part[...] = (jnp.dot(score_grads, query_stack[...], preferred_element_type=f32) * scale).astype(bf)
    to_below(lambda other, side, device: send(VGRAD_C, device, value_part.at[half(side)], vgrad_column.at[member]))
    for _, peer, device in farthest_first(plane_back):
        send(KGRAD_P, device, key_part.at[half(lax.rem(peer, 2))], kgrad_plane.at[place])
    vgrad_column[member] = value_part[half(core), :]
    kgrad_plane[place] = key_part[half(core), :]
    settle()
    sent += [(VGRAD_C, BELOW, vgrad_column), (KGRAD_P, PLANE, kgrad_plane)]
    query_acc[...] += query_share(score_grads, key_tile, scale)
    for head in range(heads):
        query_grad_ref[:, pl.ds(head * head_width, head_width)] = query_acc[
            pl.ds(head * block_rows, block_rows), :
        ]

    def owner_sum(owner, targets, held):
        terms = [jnp.where(aimed == owner, held[source].astype(f32), 0.0) for source, aimed in enumerate(targets)]
        for term in terms[1:]:
            terms[0] = terms[0] + term
        return terms[0].astype(bf)

    arrive(KGRAD_P, PLANE, kgrad_plane)

    def give_key(other, side, device):
        slot = other * 2 + side
        kgrad_sum[slot] = owner_sum(other * plane_count + chip * 2 + side, plane_sources, kgrad_plane)
        send(KGRAD_C, device, kgrad_sum.at[slot], kgrad_in.at[member])

    to_below(give_key)
    kgrad_in[member] = owner_sum(block, plane_sources, kgrad_plane)

    arrive(VGRAD_C, ABOVE, vgrad_column)
    for offset, peer, device in farthest_first(plane_back):
        vgrad_sum[offset] = owner_sum(line * plane_count + peer, column_sources, vgrad_column)
        send(VGRAD_P, device, vgrad_sum.at[offset], vgrad_in.at[place])
    vgrad_in[place] = owner_sum(block, column_sources, vgrad_column)
    sent += [(KGRAD_C, BELOW, kgrad_sum), (VGRAD_P, PLANE, vgrad_sum)]
    settle()

    def grown(total, halves):
        parts = halves[...].astype(f32).reshape(halves.shape[0] // 2, block_rows, head_width)
        return total + jnp.sum(parts, axis=0)

    arrive(KGRAD_C, ABOVE, kgrad_in)
    key_grad_ref[...] = grown(key_acc[...], kgrad_in)
    arrive(VGRAD_P, PLANE, vgrad_in)
    value_grad_ref[...] = grown(value_acc[...], vgrad_in)


def kernel_shards(query_rows, key_rows, value_rows, outputs, out_grads, log_totals, selected, counts):
    ka_count, pb_count = lax.axis_size("ka"), lax.axis_size("pb")
    inner = 2 if pb_count % 2 == 0 else 1
    line_count, plane_count = pb_count // inner, inner * ka_count
    column_count = 2 * line_count
    block_rows, head_width = key_rows.shape
    heads = log_totals.shape[0]
    tile = key_rows.shape
    half_rows = block_rows // 2
    part = (half_rows, head_width)
    dma = pltpu.SemaphoreType.DMA
    vmem = pl.BlockSpec(memory_space=pltpu.VMEM)
    hbm = pl.BlockSpec(memory_space=pl.ANY)
    bf, f32 = jnp.bfloat16, jnp.float32
    shapes = (query_rows.shape, key_rows.shape, value_rows.shape)
    held = pl.pallas_call(
        functools.partial(whole_kernel, ka_count, inner, line_count),
        out_shape=tuple(pltpu.VMEM(shape, f32) for shape in shapes),
        in_specs=[hbm] * 7 + [pl.BlockSpec(memory_space=pltpu.SMEM)],
        out_specs=(vmem, vmem, vmem),
        scratch_shapes=[
            pltpu.VMEM(query_rows.shape, bf),
            pltpu.VMEM(query_rows.shape, bf),
            pltpu.VMEM(query_rows.shape, bf),
            pltpu.VMEM(log_totals.shape, f32),
            pltpu.SMEM(selected.shape, jnp.int32),
            pltpu.VMEM(tile, bf),
            pltpu.VMEM(tile, bf),
            pltpu.VMEM((plane_count, *part), bf),
            pltpu.VMEM((column_count, *part), bf),
            pltpu.VMEM((column_count, *part), bf),
            pltpu.VMEM((plane_count, *part), bf),
            pltpu.VMEM((column_count, *part), bf),
            pltpu.VMEM((plane_count, *part), bf),
            pltpu.VMEM(tile, bf),
            pltpu.VMEM(tile, bf),
            pltpu.VMEM((plane_count, *part), bf),
            pltpu.VMEM((column_count, *part), bf),
            pltpu.VMEM((column_count, *part), bf),
            pltpu.VMEM((plane_count, *part), bf),
            pltpu.VMEM((column_count * half_rows, plane_count * half_rows), bf),
            pltpu.VMEM((plane_count * half_rows, column_count * half_rows), bf),
            pltpu.VMEM((column_count, *part), bf),
            pltpu.VMEM((plane_count, *part), bf),
            pltpu.VMEM((1, INFO), jnp.int32),
            pltpu.VMEM((plane_count, 1, INFO), jnp.int32),
            pltpu.VMEM((column_count, 1, INFO), jnp.int32),
            pltpu.VMEM((heads * block_rows, head_width), bf),
            pltpu.VMEM((heads * block_rows, head_width), bf),
            pltpu.VMEM((head_width, heads * block_rows), bf),
            pltpu.VMEM((head_width, heads * block_rows), bf),
            pltpu.VMEM((heads * block_rows, head_width), f32),
            pltpu.VMEM(tile, f32),
            pltpu.VMEM(tile, f32),
            dma((10,)),
            dma((10,)),
            dma((8,)),
        ],
        compiler_params=pltpu.CompilerParams(collective_id=0, has_side_effects=True),
    )(query_rows, key_rows, value_rows, outputs, out_grads, log_totals, selected, counts)
    return pl.pallas_call(
        write_kernel,
        out_shape=tuple(jax.ShapeDtypeStruct(shape, f32) for shape in shapes),
        in_specs=[vmem] * 3,
        out_specs=(hbm, hbm, hbm),
        scratch_shapes=[dma((3,))],
    )(*[pltpu.with_memory_space_constraint(part, pltpu.VMEM) for part in held])


def write_kernel(*refs):
    sources, targets, sem = refs[:3], refs[3:6], refs[6]
    stores = [pltpu.make_async_copy(*pair, sem.at[i]) for i, pair in enumerate(zip(sources, targets))]
    for store in stores:
        store.start()
    for store in stores:
        store.wait()


def fits_kernel(query_rows, key_rows, value_rows, outputs, out_grads, log_totals, selected, counts):
    pb_count, ka_count = lax.axis_size("pb"), lax.axis_size("ka")
    block_rows, head_width = key_rows.shape
    inner = 2 if pb_count % 2 == 0 else 1
    tile_bytes = 2 * block_rows * head_width
    tiles = 6 * (pb_count // inner + inner * ka_count)
    return (
        selected.shape[0] == 1
        and selected.shape[1] == 2
        and ka_count % 2 == 0
        and pb_count > inner
        and block_rows == head_width == 128
        and tiles * tile_bytes < VMEM_BUDGET
    )


def either(*arrays):
    return kernel_shards(*arrays) if fits_kernel(*arrays) else shards(*arrays)


def solution(mesh):
    return jax.shard_map(
        either,
        mesh=mesh,
        in_specs=(
            P(("pb", "ka"), None),
            P(("pb", "ka"), None),
            P(("pb", "ka"), None),
            P(("pb", "ka"), None),
            P(("pb", "ka"), None),
            P(None, ("pb", "ka")),
            P(("pb", "ka"), None),
            P(("pb", "ka")),
        ),
        out_specs=(P(("pb", "ka"), None), P(("pb", "ka"), None), P(("pb", "ka"), None)),
        check_vma=False,
    )
```
